256 devices in a mesh: ctx: 32 (over z, x_hi, core), tp: 8 (over y, x_lo).
Axes of the slice: x: 4 (x_hi: 2, x_lo: 2; x = x_hi * 2 + x_lo), y: 4, z: 8, core: 2. Of those that a mesh axis runs over, the one named last changes fastest.
Arguments:
- compressed: bfloat16 [4096, 1536], P('ctx', 'tp'), may hold values from -6 to 6
- latent: bfloat16 [4096, 576], P('ctx'), may hold values from -276 to 276
- w_uq: bfloat16 [1536, 12288], P(None, 'tp'), may hold values from -0.15625 to 0.15625
- w_uk: bfloat16 [512, 8192], P('ctx', 'tp'), may hold values from -0.5 to 0.5
- w_uv: bfloat16 [512, 8192], P('ctx', 'tp'), may hold values from -0.8984375 to 0.8984375
- span_ids: int32 [64], replicated, may hold values from 0 to 63, as said below
Outputs:
- attended: bfloat16 [4096, 8192], P('ctx', 'tp')
The draws below stay inside these ranges and needn't reach their ends.
Inputs may be any that keep to these rules, and one draw needn't show every extreme that they name: `span_ids`: entries 2 d and 2 d + 1 hold spans c and 63 - c for some c < 32, in that order; every span appears once.
All inputs are finite; a program needn't handle non-finite values.
Results may differ from the reference program's by a relative error of at most 0.0085.
The reference program's roundings to bfloat16 on the way count: a program that leaves them out, or rounds other values in their place, can miss the bound.
Values may be sent and summed in bfloat16 or wider, within the bound.
No kernel may reach another device: no remote copies, remote signals or barrier semaphores. Data moves between devices by JAX's collectives and lax.ppermute only.
A program may use at most 64 MiB of HBM per device.

```python
import jax
import jax.numpy as jnp
from jax import lax

QR = 1536
HEADS = 64
NOPE = 128
ROPE = 64
VDIM = 128
KV = 512
SPAN = 64
SPANS = 64
SEQ = 4096


def draw_span_ids(key, part):
    device_order = jax.random.permutation(key, SPANS // 2)
    paired = jnp.stack([device_order, SPANS - 1 - device_order], axis=1)
    return paired.reshape(SPANS).astype(jnp.int32)


def draw_latent(key, part):
    normal_part = jax.random.normal(jax.random.fold_in(key, 1), (SEQ, KV + ROPE), jnp.float32)
    return jnp.clip(normal_part, -4.0, 4.0).astype(jnp.bfloat16)


def level_of(stream_key, dims, cuts, least, largest):
    def one(axis_at, parts):
        steps = jax.random.uniform(jax.random.fold_in(jax.random.fold_in(stream_key, 6), axis_at), (parts,), jnp.float32, least / len(cuts), largest / len(cuts))
        return jnp.repeat(jnp.exp(steps), dims[axis_at] // parts).reshape((-1,) + (1,) * (len(dims) - axis_at - 1))

    level = one(*cuts[0])
    for cut in cuts[1:]:
        level = level * one(*cut)
    return level


def noise(own_key, shape, deviation, most, shards=(), kind=jnp.bfloat16):
    gain = level_of(own_key, shape, shards, -0.22, 0.18) if shards else 1.0
    values = jax.random.normal(own_key, shape, jnp.float32) * deviation * gain
    return jnp.minimum(jnp.maximum(values, -most), most).astype(kind)


def setup_inputs(seed: int = 0) -> dict:
    key_of = jax.random.split(jax.random.key(seed), 7)
    compressed = noise(key_of[0], (SEQ, QR), 1.0, 6.0, ((0, 32), (1, 8)))
    latent = draw_latent(jax.random.fold_in(key_of[6], 71), 0)
    w_uq = noise(key_of[2], (QR, HEADS * (NOPE + ROPE)), QR ** -0.5, 0.15625, ((1, 8),))
    w_uk = noise(key_of[3], (KV, HEADS * NOPE), NOPE ** -0.5, 0.5, ((0, 32), (1, 8)))
    w_uv = noise(key_of[4], (KV, HEADS * VDIM), 0.15, 0.8984375, ((0, 32), (1, 8)))
    span_ids = draw_span_ids(jax.random.fold_in(key_of[6], 71), 0)
    return dict(compressed=compressed, latent=latent, w_uq=w_uq, w_uk=w_uk, w_uv=w_uv, span_ids=span_ids)


def reference(compressed, latent, w_uq, w_uk, w_uv, span_ids):
    projected = jnp.dot(compressed, w_uq, preferred_element_type=jnp.float32).astype(jnp.bfloat16)
    per_head = jnp.transpose(projected.reshape(SEQ, HEADS, NOPE + ROPE), (1, 0, 2))
    key_up = jnp.transpose(w_uk.reshape(KV, HEADS, NOPE), (1, 0, 2))
    value_up = jnp.transpose(w_uv.reshape(KV, HEADS, VDIM), (1, 0, 2))
    positions = jnp.repeat(span_ids, SPAN, total_repeat_length=SEQ) * SPAN + jnp.tile(jnp.arange(SPAN, dtype=jnp.int32), SPANS)
    visible = positions[None, :] <= positions[:, None]
    softmax_scale = (NOPE + ROPE) ** -0.5

    def attend(inputs):
        head_query, head_key, head_value = inputs
        q_latent = jnp.dot(head_query[:, :NOPE], head_key.T, preferred_element_type=jnp.float32).astype(jnp.bfloat16)
        q_full = jnp.concatenate([q_latent, head_query[:, NOPE:]], axis=1)
        scores = jnp.dot(q_full, latent.T, preferred_element_type=jnp.float32) * softmax_scale
        scores = jnp.where(visible, scores, -jnp.inf)
        highest = jnp.max(scores, axis=1, keepdims=True)
        weights = jnp.exp(scores - highest)
        mixed = jnp.dot(weights.astype(jnp.bfloat16), latent[:, :KV], preferred_element_type=jnp.float32)
        mixed = (mixed / jnp.sum(weights, axis=1, keepdims=True)).astype(jnp.bfloat16)
        return jnp.dot(mixed, head_value, preferred_element_type=jnp.float32).astype(jnp.bfloat16)

    result = lax.map(attend, (per_head, key_up, value_up))
    return jnp.transpose(result, (1, 0, 2)).reshape(SEQ, HEADS * VDIM)
```

```python
import functools
import math

import jax
import jax.numpy as jnp
from jax import lax
from jax.experimental import pallas as pl
from jax.experimental.pallas import tpu as pltpu
from jax.sharding import Mesh, PartitionSpec as P

NOPE = 128
ROPE = 64
VDIM = 128
KV = 512
KW = 640
SPAN = 64
MASKED = -1e30
EXP2_SCALE = (NOPE + ROPE) ** (-0.5) * math.log2(math.e)


def gather_blocks(x, axes, count):
    copies = jnp.broadcast_to(x[None], (count,) + x.shape)
    return lax.all_to_all(copies, axes, 0, 0, tiled=True)


def other_core(x):
    return lax.ppermute(x, "core", [(0, 1), (1, 0)])


def dot_t(a, b):
    return lax.dot_general(a, b, (((1,), (1,)), ((), ())), preferred_element_type=jnp.float32)


def attend(q, keys, key_pos, q_pos, open_keys):
    s = dot_t(q, keys)
    masked = jnp.where(key_pos[:, open_keys:] <= q_pos, s[:, open_keys:], MASKED)
    if open_keys:
        s = jnp.concatenate([s[:, :open_keys], masked], axis=1)
    else:
        s = masked
    high = jnp.max(s, axis=1, keepdims=True)
    w = jnp.exp2((s - high) * EXP2_SCALE)
    total = jnp.sum(w, axis=1, keepdims=True)
    acc = jnp.dot(w.astype(jnp.bfloat16), keys[:, :KV], preferred_element_type=jnp.float32)
    return high, total, acc


def tiles(heads, tile):
    for slot in range(2):
        for row in range(0, heads * SPAN, tile):
            yield slot, row


def query_positions(scal_ref, slot, tile):
    within = lax.broadcasted_iota(jnp.int32, (tile, 1), 0) % SPAN
    return scal_ref[1 + slot] * SPAN + within


def weave(scal_ref, own_ref, oth_ref, dst_ref):
    core = scal_ref[0]
    rows = 16
    for i in range(own_ref.shape[0] // rows):
        at = pl.multiple_of((2 * i + core) * rows, rows)
        ot = pl.multiple_of((2 * i + 1 - core) * rows, rows)
        dst_ref[pl.ds(at, rows), :] = own_ref[i * rows : (i + 1) * rows, :]
        dst_ref[pl.ds(ot, rows), :] = oth_ref[i * rows : (i + 1) * rows, :]


def first_kernel(
    heads, tile, scal_ref, qn_ref, qr_ref, wko_ref, wkx_ref, key_ref, kpos_ref,
    qf_ref, m_ref, l_ref, acc_ref, wk_ref,
):
    weave(scal_ref, wko_ref, wkx_ref, wk_ref)
    for h in range(heads):
        cols = slice(h * NOPE, (h + 1) * NOPE)
        q_latent = dot_t(qn_ref[:, cols], wk_ref[:, cols]).astype(jnp.bfloat16)
        for slot in range(2):
            rows = slice(h * SPAN, (h + 1) * SPAN)
            toks = slice(slot * SPAN, (slot + 1) * SPAN)
            qf_ref[slot, rows, :KV] = q_latent[toks, :]
            qf_ref[slot, rows, KV:] = qr_ref[toks, cols]
    half = key_ref.shape[0] // 2
    for slot, row in tiles(heads, tile):
        rows = slice(row, row + tile)
        n = half if slot == 0 else 2 * half
        high, total, acc = attend(
            qf_ref[slot, rows, :], key_ref[:n, :], kpos_ref[:, :n],
            query_positions(scal_ref, slot, tile), 0 if slot == 0 else half,
        )
        m_ref[slot, rows, :] = jnp.broadcast_to(high, (tile, 128))
        l_ref[slot, rows, :] = jnp.broadcast_to(total, (tile, 128))
        acc_ref[slot, rows, :] = acc


def second_kernel(
    heads, tile, scal_ref, qf_ref, m_ref, l_ref, acc_ref, key_ref, kpos_ref, wvo_ref, wvx_ref,
    out_ref, wv_ref, mix_ref,
):
    weave(scal_ref, wvo_ref, wvx_ref, wv_ref)
    half = key_ref.shape[0] // 2
    for slot, row in tiles(heads, tile):
        rows = slice(row, row + tile)
        n = half if slot == 0 else 2 * half
        high, total, acc = attend(
            qf_ref[slot, rows, :], key_ref[:n, :], kpos_ref[:, :n],
            query_positions(scal_ref, slot, tile), 0 if slot == 0 else half,
        )
        high0 = m_ref[slot, rows, :1]
        top = jnp.maximum(high, high0)
        a0 = jnp.exp2((high0 - top) * EXP2_SCALE)
        a1 = jnp.exp2((high - top) * EXP2_SCALE)
        total = a0 * l_ref[slot, rows, :1] + a1 * total
        mixed = (a0 * acc_ref[slot, rows, :] + a1 * acc) / total
        mix_ref[slot, rows, :] = mixed.astype(jnp.bfloat16)
    for h in range(heads):
        cols = slice(h * VDIM, (h + 1) * VDIM)
        rows = slice(h * SPAN, (h + 1) * SPAN)
        both = jnp.concatenate([mix_ref[0, rows, :], mix_ref[1, rows, :]], axis=0)
        out_ref[:, cols] = jnp.dot(
            both, wv_ref[:, cols], preferred_element_type=jnp.float32
        ).astype(jnp.bfloat16)


def call(kernel, outs, scratch, flops, *args):
    specs = [pl.BlockSpec(memory_space=pltpu.SMEM)] + [
        pl.BlockSpec(memory_space=pltpu.VMEM) for _ in args[1:]
    ]
    size = sum(math.prod(a.shape) * a.dtype.itemsize for a in args)
    return pl.pallas_call(
        kernel,
        out_shape=outs,
        in_specs=specs,
        out_specs=jax.tree.map(lambda _: pl.BlockSpec(memory_space=pltpu.VMEM), outs),
        scratch_shapes=scratch,
        compiler_params=pltpu.CompilerParams(vmem_limit_bytes=48 << 20),
        cost_estimate=pl.CostEstimate(flops=flops, bytes_accessed=size, transcendentals=flops // 1000),
    )(*args)


def per_device(compressed, latent, w_uq, w_uk, w_uv, span_ids):
    toks = compressed.shape[0]
    heads = w_uk.shape[1] // NOPE
    zs, xhs, ys, xls = (lax.axis_size(a) for a in ("z", "xh", "y", "xl"))
    tps = ys * xls
    core = lax.axis_index("core")
    tp = lax.axis_index(("y", "xl"))
    ctx = lax.axis_index(("z", "xh", "core"))
    part = toks // tps

    mine = lax.dynamic_slice_in_dim(latent, tp * part, part, 0)
    mine = jnp.pad(mine, ((0, 0), (0, KW - latent.shape[1])))
    column = gather_blocks(mine, "z", zs).reshape(zs * part, KW)
    keys = gather_blocks(column, ("y", "xl", "xh"), tps * xhs).reshape(-1, KW)
    keys_x = other_core(keys)

    features = gather_blocks(compressed.T, ("y", "xl"), tps).reshape(-1, toks)
    query = lax.dot_general(
        features, w_uq, (((0,), (0,)), ((), ())), preferred_element_type=jnp.float32
    ).astype(jnp.bfloat16)
    query = query.reshape(toks, heads, NOPE + ROPE)
    q_nope = query[:, :, :NOPE].reshape(toks, heads * NOPE)
    q_rope = jnp.pad(query[:, :, NOPE:], ((0, 0), (0, 0), (0, KW - KV - ROPE)))
    q_rope = q_rope.reshape(toks, heads * (KW - KV))

    wk = gather_blocks(w_uk, ("z", "xh"), zs * xhs).reshape(-1, w_uk.shape[1])
    wk_x = other_core(wk)
    wv = gather_blocks(w_uv, ("z", "xh"), zs * xhs).reshape(-1, w_uv.shape[1])
    wv_x = other_core(wv)

    spans = span_ids.reshape(zs, xhs, 2, 2)
    quarter = SPAN // part
    base = jnp.transpose(spans, (2, 3, 1, 0)) * SPAN
    base = jnp.broadcast_to(base[:, :, None, :, :, None], (2, 2, quarter, xhs, zs, part))
    offset = (
        jnp.arange(quarter, dtype=jnp.int32)[:, None, None, None] * part
        + jnp.arange(part, dtype=jnp.int32)[None, None, None, :]
    )
    kpos = (base + offset[None, None]).reshape(2, 1, -1)
    kpos_own = lax.dynamic_index_in_dim(kpos, core, 0, keepdims=False)
    kpos_oth = lax.dynamic_index_in_dim(kpos, 1 - core, 0, keepdims=False)
    scal = jnp.concatenate([core[None], lax.dynamic_slice_in_dim(span_ids, 2 * ctx, 2)])

    rows, tile = heads * SPAN, 256
    f32, b16 = jnp.float32, jnp.bfloat16
    shape = jax.ShapeDtypeStruct
    flops = 2 * 3 * rows * (keys.shape[0] // 2) * (KW + KV)
    qf, m, l, acc = call(
        functools.partial(first_kernel, heads, tile),
        (
            shape((2, rows, KW), b16),
            shape((2, rows, 128), f32),
            shape((2, rows, 128), f32),
            shape((2, rows, KV), f32),
        ),
        [pltpu.VMEM((KV, w_uk.shape[1]), b16)],
        flops, scal, q_nope, q_rope, wk, wk_x, keys, kpos_own,
    )
    return call(
        functools.partial(second_kernel, heads, tile),
        shape((toks, heads * VDIM), b16),
        [pltpu.VMEM((KV, w_uv.shape[1]), b16), pltpu.VMEM((2, rows, KV), b16)],
        flops, scal, qf, m, l, acc, keys_x, kpos_oth, wv, wv_x,
    )


def solution(mesh):
    fine = Mesh(mesh.devices.reshape(8, 2, 2, 4, 2), ("z", "xh", "core", "y", "xl"))
    ctx, tp = ("z", "xh", "core"), ("y", "xl")
    placed = (P(ctx, tp), P(ctx, None), P(None, tp), P(ctx, tp), P(ctx, tp), P())
    return jax.shard_map(
        per_device, mesh=fine, in_specs=placed, out_specs=P(ctx, tp), check_vma=False
    )
```

```python
import functools
import math

import jax
import jax.numpy as jnp
from jax import lax
from jax.experimental import pallas as pl
from jax.experimental.pallas import tpu as pltpu
from jax.sharding import Mesh, PartitionSpec as P

NOPE = 128
ROPE = 64
VDIM = 128
KV = 512
KW = 640
SPAN = 64
LANES = 128
MASKED = -1e30
EXP2_SCALE = (NOPE + ROPE) ** (-0.5) * math.log2(math.e)


def gather_blocks(x, axes, count):
    copies = jnp.broadcast_to(x[None], (count,) + x.shape)
    return lax.all_to_all(copies, axes, 0, 0, tiled=True)


def shift(x, axis, by):
    n = lax.axis_size(axis)
    return lax.ppermute(x, axis, [(i, (i + by) % n) for i in range(n)])


def dot_t(a, b):
    return lax.dot_general(a, b, (((1,), (1,)), ((), ())), preferred_element_type=jnp.float32)


def pack_shard(latent):
    toks = latent.shape[0]
    content = latent[:, :KV].reshape(toks, KV // LANES, LANES).transpose(1, 0, 2).reshape(-1, LANES)
    rope = jnp.concatenate([latent[: toks // 2, KV:], latent[toks // 2 :, KV:]], axis=1)
    return jnp.concatenate([content, rope], axis=0)


def weave(core, own_ref, oth_ref, dst_ref):
    rows = 16
    for i in range(own_ref.shape[0] // rows):
        at = pl.multiple_of((2 * i + core) * rows, rows)
        ot = pl.multiple_of((2 * i + 1 - core) * rows, rows)
        dst_ref[pl.ds(at, rows), :] = own_ref[i * rows : (i + 1) * rows, :]
        dst_ref[pl.ds(ot, rows), :] = oth_ref[i * rows : (i + 1) * rows, :]


def load_keys(piece_refs, klo_ref, khi_ref):
    i = 0
    for piece in piece_refs:
        for j in range(piece.shape[0]):
            rows = slice(i * SPAN, (i + 1) * SPAN)
            for b in range(KV // LANES):
                cols = slice(b * LANES, (b + 1) * LANES)
                klo_ref[rows, cols] = piece[j, b * LANES : b * LANES + SPAN, :]
                khi_ref[rows, cols] = piece[j, b * LANES + SPAN : (b + 1) * LANES, :]
            klo_ref[rows, KV:] = piece[j, KV:, :]
            khi_ref[rows, KV:] = piece[j, KV:, :]
            i += 1


def key_positions(shards, span_ref, slot):
    lane = lax.broadcasted_iota(jnp.int32, (1, LANES), 1)
    rows = []
    for i in range(0, len(shards), 2):
        a, b = span_ref[2 * shards[i] + slot], span_ref[2 * shards[i + 1] + slot]
        rows.append(jnp.where(lane < SPAN, a, b) * SPAN + lane % SPAN)
    return jnp.concatenate(rows, axis=1)


def attention_kernel(layout, heads, tile, first, last, *refs):
    refs = list(refs)
    take = lambda n: [refs.pop(0) for _ in range(n)]
    idx_ref, span_ref = take(2)
    z, xh, core, slot0 = (idx_ref[i] for i in range(4))
    if first:
        qn_ref, qlo_ref, qhi_ref, wko_ref, wkx_ref = take(5)
    else:
        q0_ref, q1_ref, q2_ref, m_ref, l_ref, acc_ref = take(6)
    piece_refs = take(len(layout))
    if last:
        wvo_ref, wvx_ref = take(2)
        (out_ref,) = take(1)
        wv_ref, mix_ref = take(2)
    else:
        if first:
            q0_ref, q1_ref, q2_ref = take(3)
        mo_ref, lo_ref, acco_ref = take(3)
        if first:
            (wk_ref,) = take(1)
    klo_ref, khi_ref = take(2)

    shards = []
    for dz, which in layout:
        for dx, dc in which:
            zz = lax.rem(z + dz + 8, 8)
            xx = 1 - xh if dx else xh
            cc = 1 - core if dc else core
            shards.append((zz * 2 + xx) * 2 + cc)
    n = len(shards) * SPAN
    load_keys(piece_refs, klo_ref, khi_ref)
    pos_lo = key_positions(shards, span_ref, 0)
    pos_hi = key_positions(shards, span_ref, 1)
    within = lax.broadcasted_iota(jnp.int32, (tile, 1), 0) % SPAN

    if first:
        weave(core, wko_ref, wkx_ref, wk_ref)
        for h in range(heads):
            cols = slice(h * NOPE, (h + 1) * NOPE)
            rows = slice(h * SPAN, (h + 1) * SPAN)
            q_latent = dot_t(qn_ref[:, cols], wk_ref[:, cols]).astype(jnp.bfloat16)
            q0_ref[rows, :KV] = q_latent[:SPAN, :]
            q0_ref[rows, KV:] = qlo_ref[:SPAN, cols]
            q1_ref[rows, :KV] = q_latent[SPAN:, :]
            q1_ref[rows, KV:] = qlo_ref[SPAN:, cols]
            q2_ref[rows, :KV] = q_latent[SPAN:, :]
            q2_ref[rows, KV:] = qhi_ref[SPAN:, cols]
    if last:
        weave(core, wvo_ref, wvx_ref, wv_ref)

    for slot in range(2):
        for row in range(0, heads * SPAN, tile):
            rows = slice(row, row + tile)
            q_pos = span_ref[slot0 + slot] * SPAN + within
            if slot == 0:
                s = jnp.where(pos_lo <= q_pos, dot_t(q0_ref[rows, :], klo_ref[...]), MASKED)
            else:
                s_lo = dot_t(q1_ref[rows, :], klo_ref[...])
                s_hi = jnp.where(pos_hi <= q_pos, dot_t(q2_ref[rows, :], khi_ref[...]), MASKED)
                s = jnp.concatenate([s_lo, s_hi], axis=1)
            high = jnp.max(s, axis=1, keepdims=True)
            if not first:
                old = m_ref[slot, rows, :1]
                high = jnp.maximum(high, old)
            w = jnp.exp2((s - high) * EXP2_SCALE)
            total = jnp.sum(w, axis=1, keepdims=True)
            w = w.astype(jnp.bfloat16)
            acc = jnp.dot(w[:, :n], klo_ref[:, :KV], preferred_element_type=jnp.float32)
            if slot == 1:
                acc += jnp.dot(w[:, n:], khi_ref[:, :KV], preferred_element_type=jnp.float32)
            if not first:
                fade = jnp.exp2((old - high) * EXP2_SCALE)
                total += fade * l_ref[slot, rows, :1]
                acc += fade * acc_ref[slot, rows, :]
            if last:
                mix_ref[slot, rows, :] = (acc / total).astype(jnp.bfloat16)
            else:
                mo_ref[slot, rows, :] = jnp.broadcast_to(high, (tile, LANES))
                lo_ref[slot, rows, :] = jnp.broadcast_to(total, (tile, LANES))
                acco_ref[slot, rows, :] = acc
    if last:
        for h in range(heads):
            cols = slice(h * VDIM, (h + 1) * VDIM)
            rows = slice(h * SPAN, (h + 1) * SPAN)
            both = jnp.concatenate([mix_ref[0, rows, :], mix_ref[1, rows, :]], axis=0)
            out_ref[:, cols] = jnp.dot(
                both, wv_ref[:, cols], preferred_element_type=jnp.float32
            ).astype(jnp.bfloat16)


def attention(layout, heads, first, last, scalars, inputs, pieces, tail, cols):
    rows = heads * SPAN
    f32, b16 = jnp.float32, jnp.bfloat16
    shape = jax.ShapeDtypeStruct
    keys = sum(p.shape[0] for p in pieces) * SPAN
    state = [shape((2, rows, LANES), f32), shape((2, rows, LANES), f32), shape((2, rows, KV), f32)]
    scratch = [pltpu.VMEM((keys, KW), b16), pltpu.VMEM((keys, KW), b16)]
    aliases = {}
    if last:
        outs = [shape((2 * SPAN, cols), b16)]
        scratch = [pltpu.VMEM((KV, cols), b16), pltpu.VMEM((2, rows, KV), b16)] + scratch
    else:
        outs = list(state)
        if first:
            outs = [shape((rows, KW), b16)] * 3 + outs
            scratch = [pltpu.VMEM((KV, cols), b16)] + scratch
        else:
            aliases = {5: 0, 6: 1, 7: 2}
    args = [*scalars, *inputs, *pieces, *tail]
    flops = 2 * 3 * rows * keys * (KW + KV)
    size = sum(math.prod(a.shape) * a.dtype.itemsize for a in args)
    vmem = pl.BlockSpec(memory_space=pltpu.VMEM)
    return pl.pallas_call(
        functools.partial(attention_kernel, layout, heads, min(rows, 256), first, last),
        out_shape=outs,
        in_specs=[pl.BlockSpec(memory_space=pltpu.SMEM)] * 2 + [vmem] * (len(args) - 2),
        out_specs=[vmem] * len(outs),
        scratch_shapes=scratch,
        input_output_aliases=aliases,
        compiler_params=pltpu.CompilerParams(vmem_limit_bytes=48 << 20),
        cost_estimate=pl.CostEstimate(
            flops=flops, bytes_accessed=size, transcendentals=3 * rows * keys
        ),
    )(*args)


def per_device(compressed, latent, w_uq, w_uk, w_uv, span_ids):
    toks = compressed.shape[0]
    cols = w_uk.shape[1]
    heads = cols // NOPE
    zs, xhs, ys, xls = (lax.axis_size(a) for a in ("z", "xh", "y", "xl"))
    ctx = lax.axis_index(("z", "xh", "core"))
    idx = jnp.stack([lax.axis_index("z"), lax.axis_index("xh"), lax.axis_index("core"), 2 * ctx])

    shard = pack_shard(latent)[None]
    here = jnp.concatenate([shard, shift(shard, "xh", 1)], axis=0)
    both, first_xh, second_xh = ((0, 0), (1, 0)), ((0, 0),), ((1, 0),)
    steps = [[(0, both, here)]]
    ahead = behind = here
    for k in range(1, zs // 2):
        ahead, behind = shift(ahead, "z", 1), shift(behind, "z", -1)
        steps.append([(-k, both, ahead), (k, both, behind)])
    steps.append(
        [
            (-(zs // 2), first_xh, shift(ahead[:1], "z", 1)),
            (zs // 2, second_xh, shift(behind[1:], "z", -1)),
        ]
    )
    flip = lambda which: tuple((dx, 1) for dx, _ in which)
    steps = [
        step + [(dz, flip(which), shift(piece, "core", 1)) for dz, which, piece in step]
        for step in steps
    ]

    wk = gather_blocks(w_uk, ("z", "xh"), zs * xhs).reshape(-1, cols)
    wk_x = shift(wk, "core", 1)
    wv = gather_blocks(w_uv, ("z", "xh"), zs * xhs).reshape(-1, cols)
    wv_x = shift(wv, "core", 1)

    features = gather_blocks(compressed.T, ("y", "xl"), ys * xls).reshape(-1, toks)
    query = lax.dot_general(
        features, w_uq, (((0,), (0,)), ((), ())), preferred_element_type=jnp.float32
    ).astype(jnp.bfloat16)
    query = query.reshape(toks, heads, NOPE + ROPE)
    q_nope = query[:, :, :NOPE].reshape(toks, cols)
    q_rope = query[:, :, NOPE:]
    q_lo = jnp.pad(q_rope, ((0, 0), (0, 0), (0, ROPE))).reshape(toks, heads * LANES)
    q_hi = jnp.pad(q_rope, ((0, 0), (0, 0), (ROPE, 0))).reshape(toks, heads * LANES)

    def run(group, first, last, inputs, tail):
        group = [piece for step in group for piece in step]
        layout = tuple((dz, which) for dz, which, _ in group)
        pieces = [piece for _, _, piece in group]
        return attention(layout, heads, first, last, [idx, span_ids], inputs, pieces, tail, cols)

    state = run(steps[:3], True, False, [q_nope, q_lo, q_hi, wk, wk_x], [])
    queries, state = state[:3], state[3:]
    state = run(steps[3:4], False, False, [*queries, *state], [])
    (out,) = run(steps[4:], False, True, [*queries, *state], [wv, wv_x])
    return out


def solution(mesh):
    fine = Mesh(mesh.devices.reshape(8, 2, 2, 4, 2), ("z", "xh", "core", "y", "xl"))
    ctx, tp = ("z", "xh", "core"), ("y", "xl")
    placed = (P(ctx, tp), P(ctx, None), P(None, tp), P(ctx, tp), P(ctx, tp), P())
    return jax.shard_map(
        per_device, mesh=fine, in_specs=placed, out_specs=P(ctx, tp), check_vma=False
    )
```

```python
import functools
import math

import jax
import jax.numpy as jnp
from jax import lax
from jax.experimental import pallas as pl
from jax.experimental.pallas import tpu as pltpu
from jax.sharding import Mesh, PartitionSpec as P

NOPE = 128
ROPE = 64
VDIM = 128
KV = 512
SPAN = 64
LANES = 128
MASKED = -1e30
EXP2_SCALE = (NOPE + ROPE) ** (-0.5) * math.log2(math.e)


def gather_blocks(x, axes, count):
    copies = jnp.broadcast_to(x[None], (count,) + x.shape)
    return lax.all_to_all(copies, axes, 0, 0, tiled=True)


def after(x, *done):
    for d in done:
        x = x + d[(0,) * d.ndim] * jnp.zeros((), x.dtype)
    return x


def shift(x, axis, by):
    n = lax.axis_size(axis)
    return lax.ppermute(x, axis, [(i, (i + by) % n) for i in range(n)])


def dot(a, b):
    return jnp.dot(a, b, preferred_element_type=jnp.float32)


def dot_t(a, b):
    return lax.dot_general(a, b, (((1,), (1,)), ((), ())), preferred_element_type=jnp.float32)


def weave(xh, core, own_ref, oth_ref, dst_ref):
    rows = 16
    for i in range(own_ref.shape[0] // rows):
        pair = (i // 2) * 2 + (xh if i % 2 == 0 else 1 - xh)
        at = pl.multiple_of((2 * pair + core) * rows, rows)
        ot = pl.multiple_of((2 * pair + 1 - core) * rows, rows)
        dst_ref[pl.ds(at, rows), :] = own_ref[i * rows : (i + 1) * rows, :]
        dst_ref[pl.ds(ot, rows), :] = oth_ref[i * rows : (i + 1) * rows, :]


def load_keys(piece_refs, klo_ref, khi_ref):
    shards = [(ref, j) for ref in piece_refs for j in range(ref.shape[0])]
    for i in range(0, len(shards), 2):
        (ref_a, a), (ref_b, b) = shards[i : i + 2]
        left, right = ref_a[a], ref_b[b]
        cols = slice(i * SPAN, (i + 2) * SPAN)
        klo_ref[:, cols] = jnp.concatenate([left[:, :SPAN], right[:, :SPAN]], axis=1)
        khi_ref[:, cols] = jnp.concatenate([left[:, SPAN:], right[:, SPAN:]], axis=1)


def key_positions(shards, span_ref, slot):
    lane = lax.broadcasted_iota(jnp.int32, (1, LANES), 1)
    rows = []
    for i in range(0, len(shards), 2):
        a, b = span_ref[2 * shards[i] + slot], span_ref[2 * shards[i + 1] + slot]
        rows.append(jnp.where(lane < SPAN, a, b) * SPAN + lane % SPAN)
    return jnp.concatenate(rows, axis=1)


def attention_kernel(layout, heads, tile, first, last, *refs):
    refs = list(refs)
    take = lambda n: [refs.pop(0) for _ in range(n)]
    idx_ref, span_ref = take(2)
    z, xh, core, slot0 = (idx_ref[i] for i in range(4))
    if first:
        query_ref, wko_ref, wkx_ref = take(3)
    else:
        q_ref, m_ref, l_ref, acc_ref = take(4)
    piece_refs = take(len(layout))
    if last:
        wvo_ref, wvx_ref = take(2)
        (out_ref,) = take(1)
        wv_ref, mix_ref = take(2)
    else:
        if first:
            (q_ref,) = take(1)
        mo_ref, lo_ref, acco_ref = take(3)
        if first:
            (wk_ref,) = take(1)
    klo_ref, khi_ref = take(2)

    shards = []
    for dz, which in layout:
        for dx, dc in which:
            zz = lax.rem(z + dz + 8, 8)
            xx = 1 - xh if dx else xh
            cc = 1 - core if dc else core
            shards.append((zz * 2 + xx) * 2 + cc)
    n = len(shards) * SPAN
    load_keys(piece_refs, klo_ref, khi_ref)
    pos_lo = key_positions(shards, span_ref, 0)
    pos_hi = key_positions(shards, span_ref, 1)
    within = lax.broadcasted_iota(jnp.int32, (tile, 1), 0) % SPAN

    if first:
        weave(xh, core, wko_ref, wkx_ref, wk_ref)
        for h in range(heads):
            cols = slice(h * NOPE, (h + 1) * NOPE)
            rows = slice(h * SPAN, (h + 1) * SPAN)
            at = h * (NOPE + ROPE)
            q_latent = dot_t(query_ref[:, at : at + NOPE], wk_ref[:, cols]).astype(jnp.bfloat16)
            q_rope = query_ref[:, at + NOPE : at + NOPE + ROPE]
            for slot in range(2):
                toks = slice(slot * SPAN, (slot + 1) * SPAN)
                q_ref[slot, rows, :KV] = q_latent[toks, :]
                q_ref[slot, rows, KV:] = q_rope[toks, :]
    if last:
        weave(xh, core, wvo_ref, wvx_ref, wv_ref)

    for slot in range(2):
        for row in range(0, heads * SPAN, tile):
            rows = slice(row, row + tile)
            q_pos = span_ref[slot0 + slot] * SPAN + within
            if slot == 0:
                s = jnp.where(pos_lo <= q_pos, dot(q_ref[slot, rows, :], klo_ref[...]), MASKED)
            else:
                s_lo = dot(q_ref[slot, rows, :], klo_ref[...])
                s_hi = jnp.where(pos_hi <= q_pos, dot(q_ref[slot, rows, :], khi_ref[...]), MASKED)
                s = jnp.concatenate([s_lo, s_hi], axis=1)
            high = jnp.max(s, axis=1, keepdims=True)
            if not first:
                old = m_ref[slot, rows, :1]
                high = jnp.maximum(high, old)
            w = jnp.exp2((s - high) * EXP2_SCALE)
            total = jnp.sum(w, axis=1, keepdims=True)
            w = w.astype(jnp.bfloat16)
            acc = dot_t(w[:, :n], klo_ref[:KV, :])
            if slot == 1:
                acc += dot_t(w[:, n:], khi_ref[:KV, :])
            if not first:
                fade = jnp.exp2((old - high) * EXP2_SCALE)
                total += fade * l_ref[slot, rows, :1]
                acc += fade * acc_ref[slot, rows, :]
            if last:
                mix_ref[slot, rows, :] = (acc / total).astype(jnp.bfloat16)
            else:
                mo_ref[slot, rows, :] = jnp.broadcast_to(high, (tile, LANES))
                lo_ref[slot, rows, :] = jnp.broadcast_to(total, (tile, LANES))
                acco_ref[slot, rows, :] = acc
    if last:
        for h in range(heads):
            cols = slice(h * VDIM, (h + 1) * VDIM)
            rows = slice(h * SPAN, (h + 1) * SPAN)
            both = jnp.concatenate([mix_ref[0, rows, :], mix_ref[1, rows, :]], axis=0)
            out_ref[:, cols] = dot(both, wv_ref[:, cols]).astype(jnp.bfloat16)


def attention(layout, heads, first, last, scalars, inputs, pieces, tail, cols):
    rows = heads * SPAN
    f32, b16 = jnp.float32, jnp.bfloat16
    shape = jax.ShapeDtypeStruct
    keys = sum(p.shape[0] for p in pieces) * SPAN
    state = [shape((2, rows, LANES), f32), shape((2, rows, LANES), f32), shape((2, rows, KV), f32)]
    scratch = [pltpu.VMEM((KV + ROPE, keys), b16), pltpu.VMEM((KV + ROPE, keys), b16)]
    aliases = {}
    if last:
        outs = [shape((2 * SPAN, cols), b16)]
        scratch = [pltpu.VMEM((KV, cols), b16), pltpu.VMEM((2, rows, KV), b16)] + scratch
    else:
        outs = list(state)
        if first:
            outs = [shape((2, rows, KV + ROPE), b16)] + outs
            scratch = [pltpu.VMEM((KV, cols), b16)] + scratch
        else:
            aliases = {3: 0, 4: 1, 5: 2}
    args = [*scalars, *inputs, *pieces, *tail]
    flops = 2 * 3 * rows * keys * (KV + ROPE + KV)
    size = sum(math.prod(a.shape) * a.dtype.itemsize for a in args)
    vmem = pl.BlockSpec(memory_space=pltpu.VMEM)
    return pl.pallas_call(
        functools.partial(attention_kernel, layout, heads, min(rows, 256), first, last),
        out_shape=outs,
        in_specs=[pl.BlockSpec(memory_space=pltpu.SMEM)] * 2 + [vmem] * (len(args) - 2),
        out_specs=[vmem] * len(outs),
        scratch_shapes=scratch,
        input_output_aliases=aliases,
        compiler_params=pltpu.CompilerParams(vmem_limit_bytes=28 << 20),
        cost_estimate=pl.CostEstimate(
            flops=flops, bytes_accessed=size, transcendentals=3 * rows * keys
        ),
    )(*args)


def per_device(compressed, latent, w_uq, w_uk, w_uv, span_ids):
    toks = compressed.shape[0]
    cols = w_uk.shape[1]
    heads = cols // NOPE
    zs, ys, xls = (lax.axis_size(a) for a in ("z", "y", "xl"))
    ctx = lax.axis_index(("z", "xh", "core"))
    idx = jnp.stack([lax.axis_index("z"), lax.axis_index("xh"), lax.axis_index("core"), 2 * ctx])

    shard = latent.T[None]
    here = jnp.concatenate([shard, shift(shard, "xh", 1)], axis=0)
    both, first_xh, second_xh = ((0, 0), (1, 0)), ((0, 0),), ((1, 0),)
    steps = [[(0, both, here)]]
    ahead = behind = here
    arrived = []
    for k in range(1, zs // 2):
        ahead, behind = shift(ahead, "z", 1), shift(behind, "z", -1)
        steps.append([(-k, both, ahead), (k, both, behind)])
        arrived += [ahead, behind]
    steps.append(
        [
            (-(zs // 2), first_xh, shift(ahead[:1], "z", 1)),
            (zs // 2, second_xh, shift(behind[1:], "z", -1)),
        ]
    )
    flip = lambda which: tuple((dx, 1) for dx, _ in which)
    steps = [
        step + [(dz, flip(which), shift(piece, "core", 1)) for dz, which, piece in step]
        for step in steps
    ]

    weights = jnp.concatenate([w_uk, w_uv], axis=0)
    weights_x = shift(weights, "xh", 1)
    shard_rows = w_uk.shape[0]
    features = after(compressed.T, weights_x, here)
    features = gather_blocks(features, ("y", "xl"), ys * xls).reshape(-1, toks)
    query = lax.dot_general(
        features, w_uq, (((0,), (0,)), ((), ())), preferred_element_type=jnp.float32
    ).astype(jnp.bfloat16)
    wk = jnp.concatenate([w_uk, weights_x[:shard_rows]], axis=0)
    wk = after(wk, features, arrived[0], arrived[1])
    wk = gather_blocks(wk, "z", zs).reshape(-1, cols)
    wk_x = shift(wk, "core", 1)
    wv = jnp.concatenate([w_uv, weights_x[shard_rows:]], axis=0)
    wv = after(wv, wk, query, arrived[2], arrived[3])
    wv = gather_blocks(wv, "z", zs).reshape(-1, cols)
    wv_x = shift(wv, "core", 1)

    def run(group, first, last, inputs, tail):
        group = [piece for step in group for piece in step]
        layout = tuple((dz, which) for dz, which, _ in group)
        pieces = [piece for _, _, piece in group]
        return attention(layout, heads, first, last, [idx, span_ids], inputs, pieces, tail, cols)

    state = run(steps[:3], True, False, [query, wk, wk_x], [])
    queries, state = state[:1], state[1:]
    (out,) = run(steps[3:], False, True, [*queries, *state], [wv, wv_x])
    return out


def solution(mesh):
    fine = Mesh(mesh.devices.reshape(8, 2, 2, 4, 2), ("z", "xh", "core", "y", "xl"))
    ctx, tp = ("z", "xh", "core"), ("y", "xl")
    placed = (P(ctx, tp), P(ctx, None), P(None, tp), P(ctx, tp), P(ctx, tp), P())
    return jax.shard_map(
        per_device, mesh=fine, in_specs=placed, out_specs=P(ctx, tp), check_vma=False
    )
```

```python
import functools
import math

import jax
import jax.numpy as jnp
from jax import lax
from jax.experimental import pallas as pl
from jax.experimental.pallas import tpu as pltpu
from jax.sharding import Mesh, PartitionSpec as P

NOPE = 128
ROPE = 64
VDIM = 128
KV = 512
SPAN = 64
LANES = 128
VARIANTS = 4
MASKED = -1e30
EXP2_SCALE = (NOPE + ROPE) ** (-0.5) * math.log2(math.e)


def after(x, *done):
    for d in done:
        x = x + d[(0,) * d.ndim] * jnp.zeros((), x.dtype)
    return x


def gather_blocks(x, axes, count):
    copies = jnp.broadcast_to(x[None], (count,) + x.shape)
    return lax.all_to_all(copies, axes, 0, 0, tiled=True)


def shift(x, axis, by):
    n = lax.axis_size(axis)
    return lax.ppermute(x, axis, [(i, (i + by) % n) for i in range(n)])


def dot(a, b):
    return jnp.dot(a, b, preferred_element_type=jnp.float32)


def dot_t(a, b):
    return lax.dot_general(a, b, (((1,), (1,)), ((), ())), preferred_element_type=jnp.float32)


def weave(xh, core, own_ref, oth_ref, offset, dst_ref):
    rows = 16
    for i in range(dst_ref.shape[0] // (2 * rows)):
        pair = (i // 2) * 2 + (xh if i % 2 == 0 else 1 - xh)
        at = pl.multiple_of((2 * pair + core) * rows, rows)
        ot = pl.multiple_of((2 * pair + 1 - core) * rows, rows)
        src = slice(2 * i * rows + offset, 2 * i * rows + offset + rows)
        dst_ref[pl.ds(at, rows), :] = own_ref[src, :]
        dst_ref[pl.ds(ot, rows), :] = oth_ref[src, :]


def attend_rows(q_ref, lo_ref, hi_ref, mix_ref, c, slot, rows, variant):
    q = q_ref[slot, rows, :]
    count = lo_ref.shape[1]
    step = count // VARIANTS
    within = lax.broadcasted_iota(jnp.int32, (q.shape[0], 1), 0) % SPAN
    lane = lax.broadcasted_iota(jnp.int32, (1, step), 1)
    if slot == 0:
        open_lo, n_lo = step * variant, step * (variant + 1)
        s_lo = dot(q, lo_ref[:, :n_lo])
        seen = lane + open_lo <= c * SPAN + within
        parts = [jnp.where(seen, s_lo[:, open_lo:], MASKED)]
        if open_lo:
            parts = [s_lo[:, :open_lo]] + parts
    else:
        first = step * variant
        s_hi = dot(q, hi_ref[:, first:])
        at = lane % SPAN - (lane + first) // SPAN * SPAN
        seen = at <= within - c * SPAN
        parts = [dot(q, lo_ref[...]), jnp.where(seen, s_hi[:, :step], MASKED)]
        if first + step < count:
            parts.append(s_hi[:, step:])
    s = jnp.concatenate(parts, axis=1)
    high = jnp.max(s, axis=1, keepdims=True)
    w = jnp.exp2((s - high) * EXP2_SCALE)
    total = jnp.sum(w, axis=1, keepdims=True)
    w = w.astype(jnp.bfloat16)
    if slot == 0:
        acc = dot_t(w, lo_ref[:KV, :n_lo])
    else:
        acc = dot_t(w[:, :count], lo_ref[:KV, :]) + dot_t(w[:, count:], hi_ref[:KV, first:])
    mix_ref[slot, rows, :] = (acc / total).astype(jnp.bfloat16)


def attention_kernel(layout, heads, tile, *refs):
    refs = list(refs)
    take = lambda n: [refs.pop(0) for _ in range(n)]
    idx_ref, span_ref, query_ref, w_ref, wx_ref = take(5)
    piece_refs = take(len(layout))
    out_ref, key_ref, lo_ref, hi_ref, wk_ref, wv_ref, q_ref, mix_ref, sem = refs
    z, xh, core, slot0 = (idx_ref[i] for i in range(4))
    zs = w_ref.shape[0] // 64

    copies = []
    for (dz, which), piece in zip(layout, piece_refs):
        for j, (dx, dc) in enumerate(which):
            zz = lax.rem(z + dz + zs, zs)
            xx = 1 - xh if dx else xh
            cc = 1 - core if dc else core
            place = span_ref[2 * ((zz * 2 + xx) * 2 + cc)]
            copy = pltpu.make_async_copy(piece.at[j], key_ref.at[place], sem.at[len(copies)])
            copy.start()
            copies.append(copy)

    weave(xh, core, w_ref, wx_ref, 0, wk_ref)
    for h in range(heads):
        rows = slice(h * SPAN, (h + 1) * SPAN)
        at = h * (NOPE + ROPE)
        q_latent = dot_t(query_ref[:, at : at + NOPE], wk_ref[:, h * NOPE : (h + 1) * NOPE])
        q_latent = q_latent.astype(jnp.bfloat16)
        q_rope = query_ref[:, at + NOPE : at + NOPE + ROPE]
        for slot in range(2):
            toks = slice(slot * SPAN, (slot + 1) * SPAN)
            q_ref[slot, rows, :KV] = q_latent[toks, :]
            q_ref[slot, rows, KV:] = q_rope[toks, :]
    weave(xh, core, w_ref, wx_ref, 16, wv_ref)

    for copy in copies:
        copy.wait()
    for i in range(0, len(copies), 2):
        left, right = key_ref[i], key_ref[i + 1]
        cols = slice(i * SPAN, (i + 2) * SPAN)
        lo_ref[:, cols] = jnp.concatenate([left[:, :SPAN], right[:, :SPAN]], axis=1)
        hi_ref[:, cols] = jnp.concatenate([left[:, SPAN:], right[:, SPAN:]], axis=1)

    c = span_ref[slot0]
    group = lax.div(c, len(copies) // VARIANTS)
    for variant in range(VARIANTS):

        @pl.when(group == variant)
        def _():
            def body(i, carry):
                rows = pl.ds(pl.multiple_of(i * tile, tile), tile)
                for slot in range(2):
                    attend_rows(q_ref, lo_ref, hi_ref, mix_ref, c, slot, rows, variant)
                return carry

            lax.fori_loop(0, heads * SPAN // tile, body, 0)

    for h in range(heads):
        cols = slice(h * VDIM, (h + 1) * VDIM)
        rows = slice(h * SPAN, (h + 1) * SPAN)
        both = jnp.concatenate([mix_ref[0, rows, :], mix_ref[1, rows, :]], axis=0)
        out_ref[:, cols] = dot(both, wv_ref[:, cols]).astype(jnp.bfloat16)


def attention(layout, heads, idx, span_ids, query, w, w_x, pieces):
    rows, cols = heads * SPAN, w.shape[1]
    b16 = jnp.bfloat16
    shards = sum(p.shape[0] for p in pieces)
    args = [idx, span_ids, query, w, w_x, *pieces]
    size = sum(math.prod(a.shape) * a.dtype.itemsize for a in args)
    work = 2 * rows * shards * SPAN * 5 // 4
    vmem = pl.BlockSpec(memory_space=pltpu.VMEM)
    return pl.pallas_call(
        functools.partial(attention_kernel, layout, heads, min(rows, 256)),
        out_shape=jax.ShapeDtypeStruct((2 * SPAN, cols), b16),
        in_specs=[pl.BlockSpec(memory_space=pltpu.SMEM)] * 2
        + [vmem] * 3
        + [pl.BlockSpec(memory_space=pltpu.HBM)] * len(pieces),
        out_specs=vmem,
        scratch_shapes=[
            pltpu.VMEM((shards, KV + ROPE, 2 * SPAN), b16),
            pltpu.VMEM((KV + ROPE, shards * SPAN), b16),
            pltpu.VMEM((KV + ROPE, shards * SPAN), b16),
            pltpu.VMEM((KV, cols), b16),
            pltpu.VMEM((KV, cols), b16),
            pltpu.VMEM((2, rows, KV + ROPE), b16),
            pltpu.VMEM((2, rows, KV), b16),
            pltpu.SemaphoreType.DMA((shards,)),
        ],
        compiler_params=pltpu.CompilerParams(vmem_limit_bytes=60 << 20),
        cost_estimate=pl.CostEstimate(
            flops=2 * work * (2 * KV + ROPE), bytes_accessed=size, transcendentals=work
        ),
    )(*args)


def per_device(compressed, latent, w_uq, w_uk, w_uv, span_ids):
    toks = compressed.shape[0]
    heads = w_uk.shape[1] // NOPE
    zs, ys, xls = (lax.axis_size(a) for a in ("z", "y", "xl"))
    ctx = lax.axis_index(("z", "xh", "core"))
    idx = jnp.stack([lax.axis_index("z"), lax.axis_index("xh"), lax.axis_index("core"), 2 * ctx])

    weights = jnp.concatenate([w_uk, w_uv], axis=0)
    weights = jnp.concatenate([weights, shift(weights, "xh", 1)], axis=0)
    w = lax.all_gather(weights, "z", axis=0, tiled=True)

    features = after(compressed.T, lax.optimization_barrier(weights))
    features = gather_blocks(features, ("y", "xl"), ys * xls).reshape(-1, toks)
    query = lax.dot_general(
        features, w_uq, (((0,), (0,)), ((), ())), preferred_element_type=jnp.float32
    ).astype(jnp.bfloat16)

    shard = latent.T[None]
    here = jnp.concatenate([shard, shift(shard, "xh", 1)], axis=0)
    both, first_xh, second_xh = ((0, 0), (1, 0)), ((0, 0),), ((1, 0),)
    pieces = [(0, both, here)]
    ahead = behind = here
    for k in range(1, zs // 2):
        if k == 2:
            ahead, behind = after(ahead, features), after(behind, features)
        ahead, behind = shift(ahead, "z", 1), shift(behind, "z", -1)
        pieces += [(-k, both, ahead), (k, both, behind)]
    last = shift(after(ahead[:1], query), "z", 1), shift(after(behind[1:], query), "z", -1)
    pieces += [
        (-(zs // 2), first_xh, last[0]),
        (zs // 2, second_xh, last[1]),
    ]
    handed = [
        (dz, tuple((dx, 1) for dx, _ in which), shift(piece, "core", 1))
        for dz, which, piece in pieces
    ]
    w_x = shift(after(w, *last, *(piece for _, _, piece in handed[:-2])), "core", 1)
    pieces += handed

    layout = tuple((dz, which) for dz, which, _ in pieces)
    return attention(layout, heads, idx, span_ids, query, w, w_x, [p for _, _, p in pieces])


def solution(mesh):
    fine = Mesh(mesh.devices.reshape(8, 2, 2, 4, 2), ("z", "xh", "core", "y", "xl"))
    ctx, tp = ("z", "xh", "core"), ("y", "xl")
    placed = (P(ctx, tp), P(ctx, None), P(None, tp), P(ctx, tp), P(ctx, tp), P())
    return jax.shard_map(
        per_device, mesh=fine, in_specs=placed, out_specs=P(ctx, tp), check_vma=False
    )
```

```python
import functools
import math

import jax
import jax.numpy as jnp
from jax import lax
from jax.experimental import pallas as pl
from jax.experimental.pallas import tpu as pltpu
from jax.sharding import Mesh, PartitionSpec as P

NOPE = 128
ROPE = 64
VDIM = 128
KV = 512
SPAN = 64
LANES = 128
VARIANTS = 4
MASKED = -1e30
EXP2_SCALE = (NOPE + ROPE) ** (-0.5) * math.log2(math.e)


def gate(values, *done):
    hbm = pl.BlockSpec(memory_space=pl.ANY)
    n = len(values)
    return pl.pallas_call(
        lambda *refs: None,
        out_shape=[jax.ShapeDtypeStruct(v.shape, v.dtype) for v in values],
        in_specs=[hbm] * (n + len(done)),
        out_specs=[hbm] * n,
        input_output_aliases={i: i for i in range(n)},
        compiler_params=pltpu.CompilerParams(vmem_limit_bytes=1 << 20),
        cost_estimate=pl.CostEstimate(flops=0, bytes_accessed=0, transcendentals=0),
    )(*values, *done)


def shift(x, axis, by):
    n = lax.axis_size(axis)
    return lax.ppermute(x, axis, [(i, (i + by) % n) for i in range(n)])


def dot(a, b):
    return jnp.dot(a, b, preferred_element_type=jnp.float32)


def dot_t(a, b):
    return lax.dot_general(a, b, (((1,), (1,)), ((), ())), preferred_element_type=jnp.float32)


def by_head(w):
    rows, cols = w.shape
    return w.reshape(rows, cols // LANES, LANES).transpose(1, 0, 2).reshape(-1, LANES)


def head_rows(w_ref, at, rows):
    return jnp.concatenate([w_ref[i, at : at + rows, :] for i in range(w_ref.shape[0])], axis=0)


def attend_rows(q_ref, lo_ref, hi_ref, mix_ref, c, slot, rows, variant):
    q = q_ref[slot, rows, :]
    count = lo_ref.shape[1]
    step = count // VARIANTS
    within = lax.broadcasted_iota(jnp.int32, (q.shape[0], 1), 0) % SPAN
    lane = lax.broadcasted_iota(jnp.int32, (1, step), 1)
    if slot == 0:
        open_lo, n_lo = step * variant, step * (variant + 1)
        s_lo = dot(q, lo_ref[:, :n_lo])
        seen = lane + open_lo <= c * SPAN + within
        parts = [jnp.where(seen, s_lo[:, open_lo:], MASKED)]
        if open_lo:
            parts = [s_lo[:, :open_lo]] + parts
    else:
        first = step * variant
        s_hi = dot(q, hi_ref[:, first:])
        at = lane % SPAN - (lane + first) // SPAN * SPAN
        seen = at <= within - c * SPAN
        parts = [dot(q, lo_ref[...]), jnp.where(seen, s_hi[:, :step], MASKED)]
        if first + step < count:
            parts.append(s_hi[:, step:])
    s = jnp.concatenate(parts, axis=1)
    high = jnp.max(s, axis=1, keepdims=True)
    w = jnp.exp2((s - high) * EXP2_SCALE)
    total = jnp.sum(w, axis=1, keepdims=True)
    w = w.astype(jnp.bfloat16)
    if slot == 0:
        acc = dot_t(w, lo_ref[:KV, :n_lo])
    else:
        acc = dot_t(w[:, :count], lo_ref[:KV, :]) + dot_t(w[:, count:], hi_ref[:KV, first:])
    mix_ref[slot, rows, :] = (acc / total).astype(jnp.bfloat16)


def attention_kernel(layout, heads, tile, *refs):
    refs = list(refs)
    take = lambda n: [refs.pop(0) for _ in range(n)]
    idx_ref, span_ref, query_ref = take(3)
    piece_refs = take(len(layout))
    out_ref, key_ref, w_ref, lo_ref, hi_ref, q_ref, mix_ref, key_sem, w_sem = refs
    z, xh, core, slot0 = (idx_ref[i] for i in range(4))
    shards, latent_rows = key_ref.shape[:2]
    zs = shards // 4
    shard_rows = KV // shards

    key_copies, w_copies = [], []
    for (dz, which), piece in zip(layout, piece_refs):
        for j, (dx, dc) in enumerate(which):
            zz = lax.rem(z + dz + zs, zs)
            xx = 1 - xh if dx else xh
            cc = 1 - core if dc else core
            shard, n = (zz * 2 + xx) * 2 + cc, len(w_copies)
            w_rows = pl.ds(latent_rows, w_ref.shape[1])
            w_copies.append(
                pltpu.make_async_copy(piece.at[j, w_rows], w_ref.at[shard], w_sem.at[n])
            )
            place = span_ref[2 * shard]
            key_rows = pl.ds(0, latent_rows)
            key_copies.append(
                pltpu.make_async_copy(piece.at[j, key_rows], key_ref.at[place], key_sem.at[n])
            )
    for copy in w_copies + key_copies:
        copy.start()
    for copy in w_copies:
        copy.wait()

    for h in range(heads):
        rows = slice(h * SPAN, (h + 1) * SPAN)
        at = h * (NOPE + ROPE)
        wk = head_rows(w_ref, h * shard_rows, shard_rows)
        q_latent = dot_t(query_ref[:, at : at + NOPE], wk).astype(jnp.bfloat16)
        q_rope = query_ref[:, at + NOPE : at + NOPE + ROPE]
        for slot in range(2):
            toks = slice(slot * SPAN, (slot + 1) * SPAN)
            q_ref[slot, rows, :KV] = q_latent[toks, :]
            q_ref[slot, rows, KV:] = q_rope[toks, :]

    for copy in key_copies:
        copy.wait()
    for i in range(0, shards, 2):
        left, right = key_ref[i], key_ref[i + 1]
        cols = slice(i * SPAN, (i + 2) * SPAN)
        lo_ref[:, cols] = jnp.concatenate([left[:, :SPAN], right[:, :SPAN]], axis=1)
        hi_ref[:, cols] = jnp.concatenate([left[:, SPAN:], right[:, SPAN:]], axis=1)

    c = span_ref[slot0]
    group = lax.div(c, shards // VARIANTS)
    for variant in range(VARIANTS):

        @pl.when(group == variant)
        def _():
            def body(i, carry):
                rows = pl.ds(pl.multiple_of(i * tile, tile), tile)
                for slot in range(2):
                    attend_rows(q_ref, lo_ref, hi_ref, mix_ref, c, slot, rows, variant)
                return carry

            lax.fori_loop(0, heads * SPAN // tile, body, 0)

    for h in range(heads):
        cols = slice(h * VDIM, (h + 1) * VDIM)
        rows = slice(h * SPAN, (h + 1) * SPAN)
        both = jnp.concatenate([mix_ref[0, rows, :], mix_ref[1, rows, :]], axis=0)
        wv = head_rows(w_ref, (heads + h) * shard_rows, shard_rows)
        out_ref[:, cols] = dot(both, wv).astype(jnp.bfloat16)


def attention(layout, heads, idx, span_ids, query, pieces):
    rows, cols = heads * SPAN, heads * VDIM
    b16 = jnp.bfloat16
    shards = sum(p.shape[0] for p in pieces)
    args = [idx, span_ids, query, *pieces]
    size = sum(math.prod(a.shape) * a.dtype.itemsize for a in args)
    work = 2 * rows * shards * SPAN * 5 // 4
    vmem = pl.BlockSpec(memory_space=pltpu.VMEM)
    return pl.pallas_call(
        functools.partial(attention_kernel, layout, heads, min(rows, 256)),
        out_shape=jax.ShapeDtypeStruct((2 * SPAN, cols), b16),
        in_specs=[pl.BlockSpec(memory_space=pltpu.SMEM)] * 2
        + [vmem]
        + [pl.BlockSpec(memory_space=pltpu.HBM)] * len(pieces),
        out_specs=vmem,
        scratch_shapes=[
            pltpu.VMEM((shards, KV + ROPE, 2 * SPAN), b16),
            pltpu.VMEM((shards, pieces[0].shape[1] - KV - ROPE, LANES), b16),
            pltpu.VMEM((KV + ROPE, shards * SPAN), b16),
            pltpu.VMEM((KV + ROPE, shards * SPAN), b16),
            pltpu.VMEM((2, rows, KV + ROPE), b16),
            pltpu.VMEM((2, rows, KV), b16),
            pltpu.SemaphoreType.DMA((shards,)),
            pltpu.SemaphoreType.DMA((shards,)),
        ],
        compiler_params=pltpu.CompilerParams(vmem_limit_bytes=60 << 20),
        cost_estimate=pl.CostEstimate(
            flops=2 * work * (2 * KV + ROPE), bytes_accessed=size, transcendentals=work
        ),
    )(*args)


def per_device(compressed, latent, w_uq, w_uk, w_uv, span_ids):
    toks = compressed.shape[0]
    heads = w_uk.shape[1] // NOPE
    zs, ys, xls = (lax.axis_size(a) for a in ("z", "y", "xl"))
    ctx = lax.axis_index(("z", "xh", "core"))
    idx = jnp.stack([lax.axis_index("z"), lax.axis_index("xh"), lax.axis_index("core"), 2 * ctx])

    shard = jnp.concatenate([latent.T, by_head(w_uk), by_head(w_uv)], axis=0)[None]
    here = jnp.concatenate([shard, shift(shard, "xh", 1)], axis=0)

    copies = jnp.broadcast_to(compressed.T[None], (ys * xls,) + compressed.T.shape)
    (copies,) = gate([copies], shard)
    features = lax.all_to_all(copies, ("y", "xl"), 0, 0, tiled=True).reshape(-1, toks)
    query = lax.dot_general(
        features, w_uq, (((0,), (0,)), ((), ())), preferred_element_type=jnp.float32
    ).astype(jnp.bfloat16)

    both, first_xh, second_xh = ((0, 0), (1, 0)), ((0, 0),), ((1, 0),)
    pieces = [(0, both, here)]
    ahead = behind = here
    for k in range(1, zs // 2):
        ahead, behind = shift(ahead, "z", 1), shift(behind, "z", -1)
        if k == 1:
            ahead, behind = gate([ahead, behind], features)
        if k == 2:
            ahead, behind = gate([ahead, behind], query)
        pieces += [(-k, both, ahead), (k, both, behind)]
    pieces += [
        (-(zs // 2), first_xh, shift(ahead[:1], "z", 1)),
        (zs // 2, second_xh, shift(behind[1:], "z", -1)),
    ]
    pieces += [
        (dz, tuple((dx, 1) for dx, _ in which), shift(piece, "core", 1))
        for dz, which, piece in pieces
    ]
    layout = tuple((dz, which) for dz, which, _ in pieces)
    return attention(layout, heads, idx, span_ids, query, [p for _, _, p in pieces])


def solution(mesh):
    fine = Mesh(mesh.devices.reshape(8, 2, 2, 4, 2), ("z", "xh", "core", "y", "xl"))
    ctx, tp = ("z", "xh", "core"), ("y", "xl")
    placed = (P(ctx, tp), P(ctx, None), P(None, tp), P(ctx, tp), P(ctx, tp), P())
    return jax.shard_map(
        per_device, mesh=fine, in_specs=placed, out_specs=P(ctx, tp), check_vma=False
    )
```

```python
import functools
import math

import jax
import jax.numpy as jnp
from jax import lax
from jax.experimental import pallas as pl
from jax.experimental.pallas import tpu as pltpu
from jax.sharding import Mesh, PartitionSpec as P

NOPE = 128
ROPE = 64
VDIM = 128
KV = 512
SPAN = 64
LANES = 128
VARIANTS = 4
MASKED = -1e30
EXP2_SCALE = (NOPE + ROPE) ** (-0.5) * math.log2(math.e)


def gate(values, *done):
    hbm = pl.BlockSpec(memory_space=pl.ANY)
    n = len(values)
    return pl.pallas_call(
        lambda *refs: None,
        out_shape=[jax.ShapeDtypeStruct(v.shape, v.dtype) for v in values],
        in_specs=[hbm] * (n + len(done)),
        out_specs=[hbm] * n,
        input_output_aliases={i: i for i in range(n)},
        compiler_params=pltpu.CompilerParams(vmem_limit_bytes=1 << 20),
        cost_estimate=pl.CostEstimate(flops=0, bytes_accessed=0, transcendentals=0),
    )(*values, *done)


def shift(x, axis, by):
    n = lax.axis_size(axis)
    return lax.ppermute(x, axis, [(i, (i + by) % n) for i in range(n)])


def dot(a, b):
    return jnp.dot(a, b, preferred_element_type=jnp.float32)


def dot_t(a, b):
    return lax.dot_general(a, b, (((1,), (1,)), ((), ())), preferred_element_type=jnp.float32)


def by_head(w):
    rows, cols = w.shape
    return w.reshape(rows, cols // LANES, LANES).transpose(1, 0, 2).reshape(-1, LANES)


def head_rows(w_ref, at, rows):
    return jnp.concatenate([w_ref[i, at : at + rows, :] for i in range(w_ref.shape[0])], axis=0)


def attend_rows(q_ref, lo_ref, hi_ref, mix_ref, c, slot, rows, variant):
    q = q_ref[slot, rows, :]
    count = lo_ref.shape[1]
    step = count // VARIANTS
    within = lax.broadcasted_iota(jnp.int32, (q.shape[0], 1), 0) % SPAN
    lane = lax.broadcasted_iota(jnp.int32, (1, step), 1)
    if slot == 0:
        open_lo, n_lo = step * variant, step * (variant + 1)
        s_lo = dot(q, lo_ref[:, :n_lo])
        seen = lane + open_lo <= c * SPAN + within
        parts = [jnp.where(seen, s_lo[:, open_lo:], MASKED)]
        if open_lo:
            parts = [s_lo[:, :open_lo]] + parts
    else:
        first = step * variant
        s_hi = dot(q, hi_ref[:, first:])
        at = lane % SPAN - (lane + first) // SPAN * SPAN
        seen = at <= within - c * SPAN
        parts = [dot(q, lo_ref[...]), jnp.where(seen, s_hi[:, :step], MASKED)]
        if first + step < count:
            parts.append(s_hi[:, step:])
    s = jnp.concatenate(parts, axis=1)
    high = jnp.max(s, axis=1, keepdims=True)
    w = jnp.exp2((s - high) * EXP2_SCALE)
    total = jnp.sum(w, axis=1, keepdims=True)
    w = w.astype(jnp.bfloat16)
    if slot == 0:
        acc = dot_t(w, lo_ref[:KV, :n_lo])
    else:
        acc = dot_t(w[:, :count], lo_ref[:KV, :]) + dot_t(w[:, count:], hi_ref[:KV, first:])
    mix_ref[slot, rows, :] = (acc / total).astype(jnp.bfloat16)


def attention_kernel(layout, heads, tile, *refs):
    refs = list(refs)
    take = lambda n: [refs.pop(0) for _ in range(n)]
    idx_ref, span_ref, query_ref = take(3)
    piece_refs = take(len(layout))
    out_ref, key_ref, w_ref, lo_ref, hi_ref, q_ref, mix_ref, key_sem, w_sem = refs
    z, xh, core, slot0 = (idx_ref[i] for i in range(4))
    shards, latent_rows = key_ref.shape[:2]
    zs = shards // 4
    shard_rows = KV // shards

    key_copies, w_copies = [], []
    for (dz, which), piece in zip(layout, piece_refs):
        for j, (dx, dc) in enumerate(which):
            zz = lax.rem(z + dz + zs, zs)
            xx = 1 - xh if dx else xh
            cc = 1 - core if dc else core
            shard, n = (zz * 2 + xx) * 2 + cc, len(w_copies)
            w_rows = pl.ds(latent_rows, w_ref.shape[1])
            w_copies.append(
                pltpu.make_async_copy(piece.at[j, w_rows], w_ref.at[shard], w_sem.at[n])
            )
            place = span_ref[2 * shard]
            key_rows = pl.ds(0, latent_rows)
            key_copies.append(
                pltpu.make_async_copy(piece.at[j, key_rows], key_ref.at[place], key_sem.at[n])
            )
    for copy in w_copies + key_copies:
        copy.start()
    for copy in w_copies:
        copy.wait()

    for h in range(heads):
        rows = slice(h * SPAN, (h + 1) * SPAN)
        at = h * (NOPE + ROPE)
        wk = head_rows(w_ref, h * shard_rows, shard_rows)
        q_latent = dot_t(query_ref[:, at : at + NOPE], wk).astype(jnp.bfloat16)
        q_rope = query_ref[:, at + NOPE : at + NOPE + ROPE]
        for slot in range(2):
            toks = slice(slot * SPAN, (slot + 1) * SPAN)
            q_ref[slot, rows, :KV] = q_latent[toks, :]
            q_ref[slot, rows, KV:] = q_rope[toks, :]

    for copy in key_copies:
        copy.wait()
    for i in range(0, shards, 2):
        left, right = key_ref[i], key_ref[i + 1]
        cols = slice(i * SPAN, (i + 2) * SPAN)
        lo_ref[:, cols] = jnp.concatenate([left[:, :SPAN], right[:, :SPAN]], axis=1)
        hi_ref[:, cols] = jnp.concatenate([left[:, SPAN:], right[:, SPAN:]], axis=1)

    c = span_ref[slot0]
    group = lax.div(c, shards // VARIANTS)
    for variant in range(VARIANTS):

        @pl.when(group == variant)
        def _():
            def body(i, carry):
                rows = pl.ds(pl.multiple_of(i * tile, tile), tile)
                for slot in range(2):
                    attend_rows(q_ref, lo_ref, hi_ref, mix_ref, c, slot, rows, variant)
                return carry

            lax.fori_loop(0, heads * SPAN // tile, body, 0)

    for h in range(heads):
        cols = slice(h * VDIM, (h + 1) * VDIM)
        rows = slice(h * SPAN, (h + 1) * SPAN)
        both = jnp.concatenate([mix_ref[0, rows, :], mix_ref[1, rows, :]], axis=0)
        wv = head_rows(w_ref, (heads + h) * shard_rows, shard_rows)
        out_ref[:, cols] = dot(both, wv).astype(jnp.bfloat16)


def attention(layout, heads, idx, span_ids, query, pieces):
    rows, cols = heads * SPAN, heads * VDIM
    b16 = jnp.bfloat16
    shards = sum(p.shape[0] for p in pieces)
    args = [idx, span_ids, query, *pieces]
    size = sum(math.prod(a.shape) * a.dtype.itemsize for a in args)
    work = 2 * rows * shards * SPAN * 5 // 4
    vmem = pl.BlockSpec(memory_space=pltpu.VMEM)
    return pl.pallas_call(
        functools.partial(attention_kernel, layout, heads, min(rows, 256)),
        out_shape=jax.ShapeDtypeStruct((2 * SPAN, cols), b16),
        in_specs=[pl.BlockSpec(memory_space=pltpu.SMEM)] * 2
        + [vmem]
        + [pl.BlockSpec(memory_space=pltpu.HBM)] * len(pieces),
        out_specs=vmem,
        scratch_shapes=[
            pltpu.VMEM((shards, KV + ROPE, 2 * SPAN), b16),
            pltpu.VMEM((shards, pieces[0].shape[1] - KV - ROPE, LANES), b16),
            pltpu.VMEM((KV + ROPE, shards * SPAN), b16),
            pltpu.VMEM((KV + ROPE, shards * SPAN), b16),
            pltpu.VMEM((2, rows, KV + ROPE), b16),
            pltpu.VMEM((2, rows, KV), b16),
            pltpu.SemaphoreType.DMA((shards,)),
            pltpu.SemaphoreType.DMA((shards,)),
        ],
        compiler_params=pltpu.CompilerParams(vmem_limit_bytes=60 << 20),
        cost_estimate=pl.CostEstimate(
            flops=2 * work * (2 * KV + ROPE), bytes_accessed=size, transcendentals=work
        ),
    )(*args)


def per_device(compressed, latent, w_uq, w_uk, w_uv, span_ids):
    toks = compressed.shape[0]
    heads = w_uk.shape[1] // NOPE
    zs, ys, xls = (lax.axis_size(a) for a in ("z", "y", "xl"))
    ctx = lax.axis_index(("z", "xh", "core"))
    idx = jnp.stack([lax.axis_index("z"), lax.axis_index("xh"), lax.axis_index("core"), 2 * ctx])

    own = latent.T
    across = lax.ppermute(own, ("xh", "xl"), [(0, 3), (3, 0), (1, 2), (2, 1)])
    weights = jnp.concatenate([by_head(w_uk), by_head(w_uv)], axis=0)
    weights_x = shift(weights, "xh", 1)
    here = jnp.stack(
        [jnp.concatenate([own, weights], axis=0), jnp.concatenate([across, weights_x], axis=0)]
    )

    copies = jnp.broadcast_to(compressed.T[None], (ys * xls,) + compressed.T.shape)
    (copies,) = gate([copies], weights)
    features = lax.all_to_all(copies, ("y", "xl"), 0, 0, tiled=True).reshape(-1, toks)
    query = lax.dot_general(
        features, w_uq, (((0,), (0,)), ((), ())), preferred_element_type=jnp.float32
    ).astype(jnp.bfloat16)

    both, first_xh, second_xh = ((0, 0), (1, 0)), ((0, 0),), ((1, 0),)
    pieces = [(0, both, here)]
    ahead = behind = here
    for k in range(1, zs // 2):
        ahead, behind = shift(ahead, "z", 1), shift(behind, "z", -1)
        if k == 1:
            ahead, behind = gate([ahead, behind], query)
        pieces += [(-k, both, ahead), (k, both, behind)]
    pieces += [
        (-(zs // 2), first_xh, shift(ahead[:1], "z", 1)),
        (zs // 2, second_xh, shift(behind[1:], "z", -1)),
    ]
    pieces += [
        (dz, tuple((dx, 1) for dx, _ in which), shift(piece, "core", 1))
        for dz, which, piece in pieces
    ]
    layout = tuple((dz, which) for dz, which, _ in pieces)
    return attention(layout, heads, idx, span_ids, query, [p for _, _, p in pieces])


def solution(mesh):
    fine = Mesh(mesh.devices.reshape(8, 2, 2, 4, 2), ("z", "xh", "core", "y", "xl"))
    ctx, tp = ("z", "xh", "core"), ("y", "xl")
    placed = (P(ctx, tp), P(ctx, None), P(None, tp), P(ctx, tp), P(ctx, tp), P())
    return jax.shard_map(
        per_device, mesh=fine, in_specs=placed, out_specs=P(ctx, tp), check_vma=False
    )
```

```python
import functools
import math

import jax
import jax.numpy as jnp
from jax import lax
from jax.experimental import pallas as pl
from jax.experimental.pallas import tpu as pltpu
from jax.sharding import Mesh, PartitionSpec as P

NOPE = 128
ROPE = 64
VDIM = 128
KV = 512
SPAN = 64
LANES = 128
VARIANTS = 4
PREPARE_VMEM = 40 << 20
ATTENTION_VMEM = 28 << 20
MASKED = -1e30
EXP2_SCALE = (NOPE + ROPE) ** (-0.5) * math.log2(math.e)


def gate(values, *done):
    hbm = pl.BlockSpec(memory_space=pl.ANY)
    n = len(values)
    return pl.pallas_call(
        lambda *refs: None,
        out_shape=[jax.ShapeDtypeStruct(v.shape, v.dtype) for v in values],
        in_specs=[hbm] * (n + len(done)),
        out_specs=[hbm] * n,
        input_output_aliases={i: i for i in range(n)},
        compiler_params=pltpu.CompilerParams(vmem_limit_bytes=1 << 20),
        cost_estimate=pl.CostEstimate(flops=0, bytes_accessed=0, transcendentals=0),
    )(*values, *done)


def shift(x, axis, by):
    n = lax.axis_size(axis)
    return lax.ppermute(x, axis, [(i, (i + by) % n) for i in range(n)])


def dot(a, b):
    return jnp.dot(a, b, preferred_element_type=jnp.float32)


def dot_t(a, b):
    return lax.dot_general(a, b, (((1,), (1,)), ((), ())), preferred_element_type=jnp.float32)


def by_head(w):
    rows, cols = w.shape
    return w.reshape(rows, cols // LANES, LANES).transpose(1, 0, 2).reshape(-1, LANES)


def head_rows(w_ref, at, rows):
    return jnp.concatenate([w_ref[i, at : at + rows, :] for i in range(w_ref.shape[0])], axis=0)


def attend_rows(q_ref, lo_ref, hi_ref, mix_ref, c, slot, rows, variant):
    q = q_ref[slot, rows, :]
    count = lo_ref.shape[1]
    step = count // VARIANTS
    within = lax.broadcasted_iota(jnp.int32, (q.shape[0], 1), 0) % SPAN
    lane = lax.broadcasted_iota(jnp.int32, (1, step), 1)
    if slot == 0:
        open_lo, n_lo = step * variant, step * (variant + 1)
        s_lo = dot(q, lo_ref[:, :n_lo])
        seen = lane + open_lo <= c * SPAN + within
        parts = [jnp.where(seen, s_lo[:, open_lo:], MASKED)]
        if open_lo:
            parts = [s_lo[:, :open_lo]] + parts
    else:
        first = step * variant
        s_hi = dot(q, hi_ref[:, first:])
        at = lane % SPAN - (lane + first) // SPAN * SPAN
        seen = at <= within - c * SPAN
        parts = [dot(q, lo_ref[...]), jnp.where(seen, s_hi[:, :step], MASKED)]
        if first + step < count:
            parts.append(s_hi[:, step:])
    s = jnp.concatenate(parts, axis=1)
    high = jnp.max(s, axis=1, keepdims=True)
    w = jnp.exp2((s - high) * EXP2_SCALE)
    total = jnp.sum(w, axis=1, keepdims=True)
    w = w.astype(jnp.bfloat16)
    if slot == 0:
        acc = dot_t(w, lo_ref[:KV, :n_lo])
    else:
        acc = dot_t(w[:, :count], lo_ref[:KV, :]) + dot_t(w[:, count:], hi_ref[:KV, first:])
    mix_ref[slot, rows, :] = (acc / total).astype(jnp.bfloat16)


def fetch(layout, idx_ref, span_ref, piece_refs, key_ref, w_ref, key_sem, w_sem):
    z, xh, core = (idx_ref[i] for i in range(3))
    shards, latent_rows = key_ref.shape[:2]
    zs = shards // 4
    key_copies, w_copies, places = [], [], []
    for (dz, which), piece in zip(layout, piece_refs):
        for j, (dx, dc) in enumerate(which):
            zz = lax.rem(z + dz + zs, zs)
            xx = 1 - xh if dx else xh
            cc = 1 - core if dc else core
            shard, n = (zz * 2 + xx) * 2 + cc, len(places)
            places.append(span_ref[2 * shard])
            w_rows = pl.ds(latent_rows, w_ref.shape[1])
            w_copies.append(
                pltpu.make_async_copy(piece.at[j, w_rows], w_ref.at[shard], w_sem.at[n])
            )
            key_rows = pl.ds(0, latent_rows)
            key_copies.append(
                pltpu.make_async_copy(piece.at[j, key_rows], key_ref.at[places[n]], key_sem.at[n])
            )
    for copy in w_copies + key_copies:
        copy.start()
    return key_copies, w_copies, places


def pair_up(key_ref, lo_ref, hi_ref, pair):
    left, right = key_ref[2 * pair], key_ref[2 * pair + 1]
    cols = pl.ds(pl.multiple_of(pair * 2 * SPAN, 2 * SPAN), 2 * SPAN)
    lo_ref[:, cols] = jnp.concatenate([left[:, :SPAN], right[:, :SPAN]], axis=1)
    hi_ref[:, cols] = jnp.concatenate([left[:, SPAN:], right[:, SPAN:]], axis=1)


def prepare_kernel(layout, *refs):
    idx_ref, span_ref, *piece_refs = refs[: 2 + len(layout)]
    key_ref, w_ref, lo_ref, hi_ref, token_ref, key_sem, w_sem = refs[2 + len(layout) :]
    token_ref[...] = jnp.zeros_like(token_ref)
    key_copies, w_copies, _ = fetch(
        layout, idx_ref, span_ref, piece_refs, key_ref, w_ref, key_sem, w_sem
    )
    for copy in key_copies:
        copy.wait()
    for pair in range(key_ref.shape[0] // 2):
        pair_up(key_ref, lo_ref, hi_ref, pair)
    for copy in w_copies:
        copy.wait()


def attention_kernel(layout, heads, tile, *refs):
    idx_ref, span_ref, query_ref, _, _, _, _, *refs = refs
    piece_refs, refs = refs[: len(layout)], refs[len(layout) :]
    out_ref, key_ref, w_ref, lo_ref, hi_ref, q_ref, mix_ref, key_sem, w_sem = refs
    shards = key_ref.shape[0]
    shard_rows = KV // shards
    key_copies, w_copies, places = fetch(
        layout, idx_ref, span_ref, piece_refs, key_ref, w_ref, key_sem, w_sem
    )
    for copy in w_copies:
        copy.wait()

    for h in range(heads):
        rows = slice(h * SPAN, (h + 1) * SPAN)
        at = h * (NOPE + ROPE)
        wk = head_rows(w_ref, h * shard_rows, shard_rows)
        q_latent = dot_t(query_ref[:, at : at + NOPE], wk).astype(jnp.bfloat16)
        q_rope = query_ref[:, at + NOPE : at + NOPE + ROPE]
        for slot in range(2):
            toks = slice(slot * SPAN, (slot + 1) * SPAN)
            q_ref[slot, rows, :KV] = q_latent[toks, :]
            q_ref[slot, rows, KV:] = q_rope[toks, :]

    for copy in key_copies:
        copy.wait()
    for place in places:
        pair_up(key_ref, lo_ref, hi_ref, lax.div(place, 2))

    c = span_ref[idx_ref[3]]
    group = lax.div(c, shards // VARIANTS)
    for variant in range(VARIANTS):

        @pl.when(group == variant)
        def _():
            def body(i, carry):
                rows = pl.ds(pl.multiple_of(i * tile, tile), tile)
                for slot in range(2):
                    attend_rows(q_ref, lo_ref, hi_ref, mix_ref, c, slot, rows, variant)
                return carry

            lax.fori_loop(0, heads * SPAN // tile, body, 0)

    for h in range(heads):
        cols = slice(h * VDIM, (h + 1) * VDIM)
        rows = slice(h * SPAN, (h + 1) * SPAN)
        both = jnp.concatenate([mix_ref[0, rows, :], mix_ref[1, rows, :]], axis=0)
        wv = head_rows(w_ref, (heads + h) * shard_rows, shard_rows)
        out_ref[:, cols] = dot(both, wv).astype(jnp.bfloat16)


VMEM = pl.BlockSpec(memory_space=pltpu.VMEM)
SMEM = pl.BlockSpec(memory_space=pltpu.SMEM)
ANY = pl.BlockSpec(memory_space=pl.ANY)


def nbytes(arrays):
    return sum(math.prod(a.shape) * a.dtype.itemsize for a in arrays)


def prepare(idx, span_ids, pieces):
    layout = tuple((dz, which) for dz, which, _ in pieces)
    pieces = [piece for _, _, piece in pieces]
    shards, weight_rows = span_ids.shape[0] // 2, pieces[0].shape[1] - KV - ROPE
    count = sum(p.shape[0] for p in pieces)
    held = [
        jax.ShapeDtypeStruct(shape, jnp.bfloat16)
        for shape in (
            (shards, KV + ROPE, 2 * SPAN),
            (shards, weight_rows, LANES),
            (KV + ROPE, shards * SPAN),
            (KV + ROPE, shards * SPAN),
            (16, LANES),
        )
    ]
    return pl.pallas_call(
        functools.partial(prepare_kernel, layout),
        out_shape=held,
        in_specs=[SMEM] * 2 + [ANY] * len(pieces),
        out_specs=[VMEM] * 5,
        scratch_shapes=[pltpu.SemaphoreType.DMA((count,)), pltpu.SemaphoreType.DMA((count,))],
        compiler_params=pltpu.CompilerParams(vmem_limit_bytes=PREPARE_VMEM),
        cost_estimate=pl.CostEstimate(flops=0, bytes_accessed=2 * nbytes(held), transcendentals=0),
    )(idx, span_ids, *pieces)


def attention(heads, idx, span_ids, query, held, pieces):
    layout = tuple((dz, which) for dz, which, _ in pieces)
    pieces = [piece for _, _, piece in pieces]
    rows, cols, shards = heads * SPAN, heads * VDIM, span_ids.shape[0] // 2
    count = sum(p.shape[0] for p in pieces)
    args = [idx, span_ids, query, *held, *pieces]
    work = 2 * rows * shards * SPAN * 5 // 4
    shape = jax.ShapeDtypeStruct
    out, *_ = pl.pallas_call(
        functools.partial(attention_kernel, layout, heads, min(rows, 256)),
        out_shape=[shape((2 * SPAN, cols), query.dtype), *[shape(a.shape, a.dtype) for a in held]],
        in_specs=[SMEM] * 2 + [VMEM] * 5 + [ANY] * len(pieces),
        out_specs=[VMEM] * 5,
        input_output_aliases={3 + i: 1 + i for i in range(4)},
        scratch_shapes=[
            pltpu.VMEM((2, rows, KV + ROPE), query.dtype),
            pltpu.VMEM((2, rows, KV), query.dtype),
            pltpu.SemaphoreType.DMA((count,)),
            pltpu.SemaphoreType.DMA((count,)),
        ],
        compiler_params=pltpu.CompilerParams(vmem_limit_bytes=ATTENTION_VMEM),
        cost_estimate=pl.CostEstimate(
            flops=2 * work * (2 * KV + ROPE), bytes_accessed=nbytes(args), transcendentals=work
        ),
    )(*args)
    return out


def per_device(compressed, latent, w_uq, w_uk, w_uv, span_ids):
    toks = compressed.shape[0]
    heads = w_uk.shape[1] // NOPE
    zs, ys, xls = (lax.axis_size(a) for a in ("z", "y", "xl"))
    ctx = lax.axis_index(("z", "xh", "core"))
    idx = jnp.stack([lax.axis_index("z"), lax.axis_index("xh"), lax.axis_index("core"), 2 * ctx])

    own = latent.T
    across = lax.ppermute(own, ("xh", "xl"), [(0, 3), (3, 0), (1, 2), (2, 1)])
    weights = jnp.concatenate([by_head(w_uk), by_head(w_uv)], axis=0)
    weights_x = shift(weights, "xh", 1)
    here = jnp.stack(
        [jnp.concatenate([own, weights], axis=0), jnp.concatenate([across, weights_x], axis=0)]
    )

    copies = jnp.broadcast_to(compressed.T[None], (ys * xls,) + compressed.T.shape)
    (copies,) = gate([copies], here)
    features = lax.all_to_all(copies, ("y", "xl"), 0, 0, tiled=True).reshape(-1, toks)
    query = lax.dot_general(
        features, w_uq, (((0,), (0,)), ((), ())), preferred_element_type=jnp.float32
    ).astype(jnp.bfloat16)

    both, first_xh, second_xh = ((0, 0), (1, 0)), ((0, 0),), ((1, 0),)
    pieces = [(0, both, here)]
    ahead = behind = here
    for k in range(1, zs // 2):
        ahead, behind = shift(ahead, "z", 1), shift(behind, "z", -1)
        if k == 2:
            ahead, behind = gate([ahead, behind], query)
        pieces += [(-k, both, ahead), (k, both, behind)]
    hand = lambda some: [
        (dz, tuple((dx, 1) for dx, _ in which), shift(piece, "core", 1))
        for dz, which, piece in some
    ]
    early = pieces + hand(pieces)
    last = [shift(ahead[:1], "z", 1), shift(behind[1:], "z", -1)]
    *held, token = prepare(idx, span_ids, early)
    last = gate(last, token)
    late = [(-(zs // 2), first_xh, last[0]), (zs // 2, second_xh, last[1])]
    return attention(heads, idx, span_ids, query, held, late + hand(late))


def solution(mesh):
    fine = Mesh(mesh.devices.reshape(8, 2, 2, 4, 2), ("z", "xh", "core", "y", "xl"))
    ctx, tp = ("z", "xh", "core"), ("y", "xl")
    placed = (P(ctx, tp), P(ctx, None), P(None, tp), P(ctx, tp), P(ctx, tp), P())
    return jax.shard_map(
        per_device, mesh=fine, in_specs=placed, out_specs=P(ctx, tp), check_vma=False
    )
```

```python
import functools
import math

import jax
import jax.numpy as jnp
from jax import lax
from jax.experimental import pallas as pl
from jax.experimental.pallas import tpu as pltpu
from jax.sharding import Mesh, PartitionSpec as P

NOPE = 128
ROPE = 64
VDIM = 128
KV = 512
SPAN = 64
LANES = 128
VARIANTS = 4
MASKED = -1e30
EXP2_SCALE = (NOPE + ROPE) ** (-0.5) * math.log2(math.e)


def gate(values, *done):
    hbm = pl.BlockSpec(memory_space=pl.ANY)
    n = len(values)
    return pl.pallas_call(
        lambda *refs: None,
        out_shape=[jax.ShapeDtypeStruct(v.shape, v.dtype) for v in values],
        in_specs=[hbm] * (n + len(done)),
        out_specs=[hbm] * n,
        input_output_aliases={i: i for i in range(n)},
        compiler_params=pltpu.CompilerParams(vmem_limit_bytes=1 << 20),
        cost_estimate=pl.CostEstimate(flops=0, bytes_accessed=0, transcendentals=0),
    )(*values, *done)


def shift(x, axis, by):
    n = lax.axis_size(axis)
    return lax.ppermute(x, axis, [(i, (i + by) % n) for i in range(n)])


def dot(a, b):
    return jnp.dot(a, b, preferred_element_type=jnp.float32)


def dot_t(a, b):
    return lax.dot_general(a, b, (((1,), (1,)), ((), ())), preferred_element_type=jnp.float32)


def by_head(w):
    rows, cols = w.shape
    return w.reshape(rows, cols // LANES, LANES).transpose(1, 0, 2).reshape(-1, LANES)


def head_rows(w_ref, which, at, rows):
    shards = range(w_ref.shape[1])
    return jnp.concatenate([w_ref[which, i, at : at + rows, :] for i in shards], axis=0)


def attend_rows(q_ref, lo_ref, hi_ref, mix_ref, c, slot, rows, variant):
    q = q_ref[slot, rows, :]
    count = lo_ref.shape[1]
    step = count // VARIANTS
    within = lax.broadcasted_iota(jnp.int32, (q.shape[0], 1), 0) % SPAN
    lane = lax.broadcasted_iota(jnp.int32, (1, step), 1)
    if slot == 0:
        open_lo, n_lo = step * variant, step * (variant + 1)
        s_lo = dot(q, lo_ref[:, :n_lo])
        seen = lane + open_lo <= c * SPAN + within
        parts = [jnp.where(seen, s_lo[:, open_lo:], MASKED)]
        if open_lo:
            parts = [s_lo[:, :open_lo]] + parts
    else:
        first = step * variant
        s_hi = dot(q, hi_ref[:, first:])
        at = lane % SPAN - (lane + first) // SPAN * SPAN
        seen = at <= within - c * SPAN
        parts = [dot(q, lo_ref[...]), jnp.where(seen, s_hi[:, :step], MASKED)]
        if first + step < count:
            parts.append(s_hi[:, step:])
    s = jnp.concatenate(parts, axis=1)
    high = jnp.max(s, axis=1, keepdims=True)
    w = jnp.exp2((s - high) * EXP2_SCALE)
    total = jnp.sum(w, axis=1, keepdims=True)
    w = w.astype(jnp.bfloat16)
    if slot == 0:
        acc = dot_t(w, lo_ref[:KV, :n_lo])
    else:
        acc = dot_t(w[:, :count], lo_ref[:KV, :]) + dot_t(w[:, count:], hi_ref[:KV, first:])
    mix_ref[slot, rows, :] = (acc / total).astype(jnp.bfloat16)


def attention_kernel(layout, heads, tile, *refs):
    refs = list(refs)
    take = lambda n: [refs.pop(0) for _ in range(n)]
    idx_ref, span_ref, query_ref = take(3)
    piece_refs = take(len(layout))
    out_ref, key_ref, w_ref, lo_ref, hi_ref, q_ref, mix_ref, key_sem, w_sem = refs
    z, xh, core, slot0 = (idx_ref[i] for i in range(4))
    shards, latent_rows = key_ref.shape[:2]
    zs = shards // 4
    shard_rows = KV // shards

    key_copies, wk_copies, wv_copies = [], [], []
    for (dz, which), piece in zip(layout, piece_refs):
        for j, (dx, dc) in enumerate(which):
            zz = lax.rem(z + dz + zs, zs)
            xx = 1 - xh if dx else xh
            cc = 1 - core if dc else core
            shard, n = (zz * 2 + xx) * 2 + cc, len(key_copies)
            rows = w_ref.shape[2]
            for i, w_copies in enumerate((wk_copies, wv_copies)):
                src = piece.at[j, pl.ds(latent_rows + i * rows, rows)]
                w_copies.append(
                    pltpu.make_async_copy(src, w_ref.at[i, shard], w_sem.at[i, n])
                )
            place = span_ref[2 * shard]
            key_rows = pl.ds(0, latent_rows)
            key_copies.append(
                pltpu.make_async_copy(piece.at[j, key_rows], key_ref.at[place], key_sem.at[n])
            )
    for copy in wk_copies + key_copies + wv_copies:
        copy.start()
    for copy in wk_copies:
        copy.wait()

    for h in range(heads):
        rows = slice(h * SPAN, (h + 1) * SPAN)
        at = h * (NOPE + ROPE)
        wk = head_rows(w_ref, 0, h * shard_rows, shard_rows)
        q_latent = dot_t(query_ref[:, at : at + NOPE], wk).astype(jnp.bfloat16)
        q_rope = query_ref[:, at + NOPE : at + NOPE + ROPE]
        for slot in range(2):
            toks = slice(slot * SPAN, (slot + 1) * SPAN)
            q_ref[slot, rows, :KV] = q_latent[toks, :]
            q_ref[slot, rows, KV:] = q_rope[toks, :]

    for copy in key_copies:
        copy.wait()
    for i in range(0, shards, 2):
        left, right = key_ref[i], key_ref[i + 1]
        cols = slice(i * SPAN, (i + 2) * SPAN)
        lo_ref[:, cols] = jnp.concatenate([left[:, :SPAN], right[:, :SPAN]], axis=1)
        hi_ref[:, cols] = jnp.concatenate([left[:, SPAN:], right[:, SPAN:]], axis=1)

    c = span_ref[slot0]
    group = lax.div(c, shards // VARIANTS)
    for variant in range(VARIANTS):

        @pl.when(group == variant)
        def _():
            def body(i, carry):
                rows = pl.ds(pl.multiple_of(i * tile, tile), tile)
                for slot in range(2):
                    attend_rows(q_ref, lo_ref, hi_ref, mix_ref, c, slot, rows, variant)
                return carry

            lax.fori_loop(0, heads * SPAN // tile, body, 0)

    for copy in wv_copies:
        copy.wait()
    for h in range(heads):
        cols = slice(h * VDIM, (h + 1) * VDIM)
        rows = slice(h * SPAN, (h + 1) * SPAN)
        both = jnp.concatenate([mix_ref[0, rows, :], mix_ref[1, rows, :]], axis=0)
        wv = head_rows(w_ref, 1, h * shard_rows, shard_rows)
        out_ref[:, cols] = dot(both, wv).astype(jnp.bfloat16)


def attention(layout, heads, idx, span_ids, query, pieces):
    rows, cols = heads * SPAN, heads * VDIM
    b16 = jnp.bfloat16
    shards = sum(p.shape[0] for p in pieces)
    args = [idx, span_ids, query, *pieces]
    size = sum(math.prod(a.shape) * a.dtype.itemsize for a in args)
    work = 2 * rows * shards * SPAN * 5 // 4
    vmem = pl.BlockSpec(memory_space=pltpu.VMEM)
    return pl.pallas_call(
        functools.partial(attention_kernel, layout, heads, min(rows, 256)),
        out_shape=jax.ShapeDtypeStruct((2 * SPAN, cols), b16),
        in_specs=[pl.BlockSpec(memory_space=pltpu.SMEM)] * 2
        + [vmem]
        + [pl.BlockSpec(memory_space=pltpu.HBM)] * len(pieces),
        out_specs=vmem,
        scratch_shapes=[
            pltpu.VMEM((shards, KV + ROPE, 2 * SPAN), b16),
            pltpu.VMEM((2, shards, (pieces[0].shape[1] - KV - ROPE) // 2, LANES), b16),
            pltpu.VMEM((KV + ROPE, shards * SPAN), b16),
            pltpu.VMEM((KV + ROPE, shards * SPAN), b16),
            pltpu.VMEM((2, rows, KV + ROPE), b16),
            pltpu.VMEM((2, rows, KV), b16),
            pltpu.SemaphoreType.DMA((shards,)),
            pltpu.SemaphoreType.DMA((2, shards)),
        ],
        compiler_params=pltpu.CompilerParams(vmem_limit_bytes=60 << 20),
        cost_estimate=pl.CostEstimate(
            flops=2 * work * (2 * KV + ROPE), bytes_accessed=size, transcendentals=work
        ),
    )(*args)


def per_device(compressed, latent, w_uq, w_uk, w_uv, span_ids):
    toks = compressed.shape[0]
    heads = w_uk.shape[1] // NOPE
    zs, ys, xls = (lax.axis_size(a) for a in ("z", "y", "xl"))
    ctx = lax.axis_index(("z", "xh", "core"))
    idx = jnp.stack([lax.axis_index("z"), lax.axis_index("xh"), lax.axis_index("core"), 2 * ctx])

    own = latent.T
    across = lax.ppermute(own, ("xh", "xl"), [(0, 3), (3, 0), (1, 2), (2, 1)])
    weights = jnp.concatenate([by_head(w_uk), by_head(w_uv)], axis=0)
    weights_x = shift(weights, "xh", 1)
    here = jnp.stack(
        [jnp.concatenate([own, weights], axis=0), jnp.concatenate([across, weights_x], axis=0)]
    )

    copies = jnp.broadcast_to(compressed.T[None], (ys * xls,) + compressed.T.shape)
    (copies,) = gate([copies], here)
    features = lax.all_to_all(copies, ("y", "xl"), 0, 0, tiled=True).reshape(-1, toks)
    query = lax.dot_general(
        features, w_uq, (((0,), (0,)), ((), ())), preferred_element_type=jnp.float32
    ).astype(jnp.bfloat16)

    both, first_xh, second_xh = ((0, 0), (1, 0)), ((0, 0),), ((1, 0),)
    hand = lambda some: [
        (dz, tuple((dx, 1) for dx, _ in which), shift(piece, "core", 1))
        for dz, which, piece in some
    ]
    half = zs // 2
    pieces = [(0, both, here)]
    ahead = behind = here
    for k in range(1, half):
        ahead, behind = shift(ahead, "z", 1), shift(behind, "z", -1)
        if k == half - 2:
            ahead, behind = gate([ahead, behind], query)
        if k < half - 1:
            pieces += [(-k, both, ahead), (k, both, behind)]
    pieces += hand(pieces)
    last = gate([ahead[:1], behind[1:]], *(piece for _, _, piece in pieces[len(pieces) // 2 :]))
    last = [shift(last[0], "z", 1), shift(last[1], "z", -1)]
    ahead, behind = gate([ahead, behind], *last)
    late = [
        (1 - half, both, ahead),
        (half - 1, both, behind),
        (-half, first_xh, last[0]),
        (half, second_xh, last[1]),
    ]
    pieces += late + hand(late)
    layout = tuple((dz, which) for dz, which, _ in pieces)
    return attention(layout, heads, idx, span_ids, query, [p for _, _, p in pieces])


def solution(mesh):
    fine = Mesh(mesh.devices.reshape(8, 2, 2, 4, 2), ("z", "xh", "core", "y", "xl"))
    ctx, tp = ("z", "xh", "core"), ("y", "xl")
    placed = (P(ctx, tp), P(ctx, None), P(None, tp), P(ctx, tp), P(ctx, tp), P())
    return jax.shard_map(
        per_device, mesh=fine, in_specs=placed, out_specs=P(ctx, tp), check_vma=False
    )
```

```python
import functools
import math

import jax
import jax.numpy as jnp
from jax import lax
from jax.experimental import pallas as pl
from jax.experimental.pallas import tpu as pltpu
from jax.sharding import Mesh, PartitionSpec as P

NOPE = 128
ROPE = 64
VDIM = 128
KV = 512
SPAN = 64
LANES = 128
VARIANTS = 4
MASKED = -1e30
EXP2_SCALE = (NOPE + ROPE) ** (-0.5) * math.log2(math.e)


def gate(values, *done):
    hbm = pl.BlockSpec(memory_space=pl.ANY)
    n = len(values)
    return pl.pallas_call(
        lambda *refs: None,
        out_shape=[jax.ShapeDtypeStruct(v.shape, v.dtype) for v in values],
        in_specs=[hbm] * (n + len(done)),
        out_specs=[hbm] * n,
        input_output_aliases={i: i for i in range(n)},
        compiler_params=pltpu.CompilerParams(vmem_limit_bytes=1 << 20),
        cost_estimate=pl.CostEstimate(flops=0, bytes_accessed=0, transcendentals=0),
    )(*values, *done)


def shift(x, axis, by):
    n = lax.axis_size(axis)
    return lax.ppermute(x, axis, [(i, (i + by) % n) for i in range(n)])


def dot(a, b):
    return jnp.dot(a, b, preferred_element_type=jnp.float32)


def dot_t(a, b):
    return lax.dot_general(a, b, (((1,), (1,)), ((), ())), preferred_element_type=jnp.float32)


def by_head(w):
    rows, cols = w.shape
    return w.reshape(rows, cols // LANES, LANES).transpose(1, 0, 2).reshape(-1, LANES)


def head_rows(w_ref, which, at, rows):
    shards = range(w_ref.shape[1])
    return jnp.concatenate([w_ref[which, i, at : at + rows, :] for i in shards], axis=0)


def attend_rows(q_ref, lo_ref, hi_ref, mix_ref, c, slot, rows, variant):
    q = q_ref[slot, rows, :]
    count = lo_ref.shape[1]
    step = count // VARIANTS
    within = lax.broadcasted_iota(jnp.int32, (q.shape[0], 1), 0) % SPAN
    lane = lax.broadcasted_iota(jnp.int32, (1, step), 1)
    if slot == 0:
        open_lo, n_lo = step * variant, step * (variant + 1)
        s_lo = dot(q, lo_ref[:, :n_lo])
        seen = lane + open_lo <= c * SPAN + within
        parts = [jnp.where(seen, s_lo[:, open_lo:], MASKED)]
        if open_lo:
            parts = [s_lo[:, :open_lo]] + parts
    else:
        first = step * variant
        s_hi = dot(q, hi_ref[:, first:])
        at = lane % SPAN - (lane + first) // SPAN * SPAN
        seen = at <= within - c * SPAN
        parts = [dot(q, lo_ref[...]), jnp.where(seen, s_hi[:, :step], MASKED)]
        if first + step < count:
            parts.append(s_hi[:, step:])
    s = jnp.concatenate(parts, axis=1)
    high = jnp.max(s, axis=1, keepdims=True)
    w = jnp.exp2((s - high) * EXP2_SCALE)
    total = jnp.sum(w, axis=1, keepdims=True)
    w = w.astype(jnp.bfloat16)
    if slot == 0:
        acc = dot_t(w, lo_ref[:KV, :n_lo])
    else:
        acc = dot_t(w[:, :count], lo_ref[:KV, :]) + dot_t(w[:, count:], hi_ref[:KV, first:])
    mix_ref[slot, rows, :] = (acc / total).astype(jnp.bfloat16)


def attention_kernel(layout, heads, tile, *refs):
    refs = list(refs)
    take = lambda n: [refs.pop(0) for _ in range(n)]
    idx_ref, span_ref, query_ref = take(3)
    piece_refs = take(len(layout))
    out_ref, key_ref, w_ref, lo_ref, hi_ref, q_ref, mix_ref, key_sem, w_sem = refs
    z, xh, core, slot0 = (idx_ref[i] for i in range(4))
    shards, latent_rows = key_ref.shape[:2]
    zs = shards // 4
    shard_rows = KV // shards

    key_copies, wk_copies, wv_copies = [], [], []
    for (dz, which), piece in zip(layout, piece_refs):
        for j, (dx, dc) in enumerate(which):
            zz = lax.rem(z + dz + zs, zs)
            xx = 1 - xh if dx else xh
            cc = 1 - core if dc else core
            shard, n = (zz * 2 + xx) * 2 + cc, len(key_copies)
            rows = w_ref.shape[2]
            for i, w_copies in enumerate((wk_copies, wv_copies)):
                src = piece.at[j, pl.ds(latent_rows + i * rows, rows)]
                w_copies.append(
                    pltpu.make_async_copy(src, w_ref.at[i, shard], w_sem.at[i, n])
                )
            place = span_ref[2 * shard]
            key_rows = pl.ds(0, latent_rows)
            key_copies.append(
                pltpu.make_async_copy(piece.at[j, key_rows], key_ref.at[place], key_sem.at[n])
            )
    for copy in wk_copies + key_copies + wv_copies:
        copy.start()
    for copy in wk_copies:
        copy.wait()

    for h in range(heads):
        rows = slice(h * SPAN, (h + 1) * SPAN)
        at = h * (NOPE + ROPE)
        wk = head_rows(w_ref, 0, h * shard_rows, shard_rows)
        q_latent = dot_t(query_ref[:, at : at + NOPE], wk).astype(jnp.bfloat16)
        q_rope = query_ref[:, at + NOPE : at + NOPE + ROPE]
        for slot in range(2):
            toks = slice(slot * SPAN, (slot + 1) * SPAN)
            q_ref[slot, rows, :KV] = q_latent[toks, :]
            q_ref[slot, rows, KV:] = q_rope[toks, :]

    for copy in key_copies:
        copy.wait()
    for i in range(0, shards, 2):
        left, right = key_ref[i], key_ref[i + 1]
        cols = slice(i * SPAN, (i + 2) * SPAN)
        lo_ref[:, cols] = jnp.concatenate([left[:, :SPAN], right[:, :SPAN]], axis=1)
        hi_ref[:, cols] = jnp.concatenate([left[:, SPAN:], right[:, SPAN:]], axis=1)

    c = span_ref[slot0]
    group = lax.div(c, shards // VARIANTS)
    for variant in range(VARIANTS):

        @pl.when(group == variant)
        def _():
            def body(i, carry):
                rows = pl.ds(pl.multiple_of(i * tile, tile), tile)
                for slot in range(2):
                    attend_rows(q_ref, lo_ref, hi_ref, mix_ref, c, slot, rows, variant)
                return carry

            lax.fori_loop(0, heads * SPAN // tile, body, 0)

    for copy in wv_copies:
        copy.wait()
    for h in range(heads):
        cols = slice(h * VDIM, (h + 1) * VDIM)
        rows = slice(h * SPAN, (h + 1) * SPAN)
        both = jnp.concatenate([mix_ref[0, rows, :], mix_ref[1, rows, :]], axis=0)
        wv = head_rows(w_ref, 1, h * shard_rows, shard_rows)
        out_ref[:, cols] = dot(both, wv).astype(jnp.bfloat16)


def attention(layout, heads, idx, span_ids, query, pieces):
    rows, cols = heads * SPAN, heads * VDIM
    b16 = jnp.bfloat16
    shards = sum(p.shape[0] for p in pieces)
    args = [idx, span_ids, query, *pieces]
    size = sum(math.prod(a.shape) * a.dtype.itemsize for a in args)
    work = 2 * rows * shards * SPAN * 5 // 4
    vmem = pl.BlockSpec(memory_space=pltpu.VMEM)
    return pl.pallas_call(
        functools.partial(attention_kernel, layout, heads, min(rows, 256)),
        out_shape=jax.ShapeDtypeStruct((2 * SPAN, cols), b16),
        in_specs=[pl.BlockSpec(memory_space=pltpu.SMEM)] * 2
        + [vmem]
        + [pl.BlockSpec(memory_space=pltpu.HBM)] * len(pieces),
        out_specs=vmem,
        scratch_shapes=[
            pltpu.VMEM((shards, KV + ROPE, 2 * SPAN), b16),
            pltpu.VMEM((2, shards, (pieces[0].shape[1] - KV - ROPE) // 2, LANES), b16),
            pltpu.VMEM((KV + ROPE, shards * SPAN), b16),
            pltpu.VMEM((KV + ROPE, shards * SPAN), b16),
            pltpu.VMEM((2, rows, KV + ROPE), b16),
            pltpu.VMEM((2, rows, KV), b16),
            pltpu.SemaphoreType.DMA((shards,)),
            pltpu.SemaphoreType.DMA((2, shards)),
        ],
        compiler_params=pltpu.CompilerParams(vmem_limit_bytes=60 << 20),
        cost_estimate=pl.CostEstimate(
            flops=2 * work * (2 * KV + ROPE), bytes_accessed=size, transcendentals=work
        ),
    )(*args)


def per_device(compressed, latent, w_uq, w_uk, w_uv, span_ids):
    toks = compressed.shape[0]
    heads = w_uk.shape[1] // NOPE
    zs, ys, xls = (lax.axis_size(a) for a in ("z", "y", "xl"))
    ctx = lax.axis_index(("z", "xh", "core"))
    idx = jnp.stack([lax.axis_index("z"), lax.axis_index("xh"), lax.axis_index("core"), 2 * ctx])

    own = latent.T
    across = lax.ppermute(own, ("xh", "xl"), [(0, 3), (3, 0), (1, 2), (2, 1)])
    weights = jnp.concatenate([by_head(w_uk), by_head(w_uv)], axis=0)
    weights_x = shift(weights, "xh", 1)
    here = jnp.stack(
        [jnp.concatenate([own, weights], axis=0), jnp.concatenate([across, weights_x], axis=0)]
    )

    copies = jnp.broadcast_to(compressed.T[None], (ys * xls,) + compressed.T.shape)
    (copies,) = gate([copies], here)
    features = lax.all_to_all(copies, ("y", "xl"), 0, 0, tiled=True).reshape(-1, toks)
    query = lax.dot_general(
        features, w_uq, (((0,), (0,)), ((), ())), preferred_element_type=jnp.float32
    ).astype(jnp.bfloat16)

    both, first_xh, second_xh = ((0, 0), (1, 0)), ((0, 0),), ((1, 0),)
    hand = lambda some: [
        (dz, tuple((dx, 1) for dx, _ in which), shift(piece, "core", 1))
        for dz, which, piece in some
    ]
    half = zs // 2
    pieces, late = [(0, both, here)], []
    ahead = behind = here
    for k in range(1, half):
        ahead, behind = shift(ahead, "z", 1), shift(behind, "z", -1)
        if k == half - 2:
            ahead, behind = gate([ahead, behind], query)
        (pieces if k < half - 2 else late).extend([(-k, both, ahead), (k, both, behind)])
    pieces += hand(pieces)
    last = gate([ahead[:1], behind[1:]], *(piece for _, _, piece in pieces[len(pieces) // 2 :]))
    moved = gate([piece for _, _, piece in late], *last)
    late = [(dz, which, piece) for (dz, which, _), piece in zip(late, moved)]
    last = [shift(last[0], "z", 1), shift(last[1], "z", -1)]
    late += [(-half, first_xh, last[0]), (half, second_xh, last[1])]
    pieces += late + hand(late)
    layout = tuple((dz, which) for dz, which, _ in pieces)
    return attention(layout, heads, idx, span_ids, query, [p for _, _, p in pieces])


def solution(mesh):
    fine = Mesh(mesh.devices.reshape(8, 2, 2, 4, 2), ("z", "xh", "core", "y", "xl"))
    ctx, tp = ("z", "xh", "core"), ("y", "xl")
    placed = (P(ctx, tp), P(ctx, None), P(None, tp), P(ctx, tp), P(ctx, tp), P())
    return jax.shard_map(
        per_device, mesh=fine, in_specs=placed, out_specs=P(ctx, tp), check_vma=False
    )
```

```python
import functools
import math

import jax
import jax.numpy as jnp
from jax import lax
from jax.experimental import pallas as pl
from jax.experimental.pallas import tpu as pltpu
from jax.sharding import Mesh, PartitionSpec as P

NOPE = 128
ROPE = 64
VDIM = 128
KV = 512
SPAN = 64
LANES = 128
VARIANTS = 4
MASKED = -1e30
EXP2_SCALE = (NOPE + ROPE) ** (-0.5) * math.log2(math.e)


def gate(values, *done):
    hbm = pl.BlockSpec(memory_space=pl.ANY)
    n = len(values)
    return pl.pallas_call(
        lambda *refs: None,
        out_shape=[jax.ShapeDtypeStruct(v.shape, v.dtype) for v in values],
        in_specs=[hbm] * (n + len(done)),
        out_specs=[hbm] * n,
        input_output_aliases={i: i for i in range(n)},
        compiler_params=pltpu.CompilerParams(vmem_limit_bytes=1 << 20),
        cost_estimate=pl.CostEstimate(flops=0, bytes_accessed=0, transcendentals=0),
    )(*values, *done)


def shift(x, axis, by):
    n = lax.axis_size(axis)
    return lax.ppermute(x, axis, [(i, (i + by) % n) for i in range(n)])


def dot(a, b):
    return jnp.dot(a, b, preferred_element_type=jnp.float32)


def dot_t(a, b):
    return lax.dot_general(a, b, (((1,), (1,)), ((), ())), preferred_element_type=jnp.float32)


def by_head(w):
    rows, cols = w.shape
    return w.reshape(rows, cols // LANES, LANES).transpose(1, 0, 2).reshape(-1, LANES)


def head_rows(w_ref, which, at, rows):
    shards = range(w_ref.shape[1])
    return jnp.concatenate([w_ref[which, i, at : at + rows, :] for i in shards], axis=0)


def attend_rows(q_ref, lo_ref, hi_ref, mix_ref, c, slot, rows, variant):
    q = q_ref[slot, rows, :]
    count = lo_ref.shape[1]
    step = count // VARIANTS
    within = lax.broadcasted_iota(jnp.int32, (q.shape[0], 1), 0) % SPAN
    lane = lax.broadcasted_iota(jnp.int32, (1, step), 1)
    if slot == 0:
        open_lo, n_lo = step * variant, step * (variant + 1)
        s_lo = dot(q, lo_ref[:, :n_lo])
        seen = lane + open_lo <= c * SPAN + within
        parts = [jnp.where(seen, s_lo[:, open_lo:], MASKED)]
        if open_lo:
            parts = [s_lo[:, :open_lo]] + parts
    else:
        first = step * variant
        s_hi = dot(q, hi_ref[:, first:])
        at = lane % SPAN - (lane + first) // SPAN * SPAN
        seen = at <= within - c * SPAN
        parts = [dot(q, lo_ref[...]), jnp.where(seen, s_hi[:, :step], MASKED)]
        if first + step < count:
            parts.append(s_hi[:, step:])
    s = jnp.concatenate(parts, axis=1)
    high = jnp.max(s, axis=1, keepdims=True)
    w = jnp.exp2((s - high) * EXP2_SCALE)
    total = jnp.sum(w, axis=1, keepdims=True)
    w = w.astype(jnp.bfloat16)
    if slot == 0:
        acc = dot_t(w, lo_ref[:KV, :n_lo])
    else:
        acc = dot_t(w[:, :count], lo_ref[:KV, :]) + dot_t(w[:, count:], hi_ref[:KV, first:])
    mix_ref[slot, rows, :] = (acc / total).astype(jnp.bfloat16)


def attention_kernel(layout, heads, tile, *refs):
    refs = list(refs)
    take = lambda n: [refs.pop(0) for _ in range(n)]
    idx_ref, span_ref, query_ref = take(3)
    piece_refs = take(len(layout))
    out_ref, key_ref, w_ref, lo_ref, hi_ref, q_ref, mix_ref, key_sem, w_sem = refs
    z, xh, core, slot0 = (idx_ref[i] for i in range(4))
    shards, latent_rows = key_ref.shape[:2]
    zs = shards // 4
    shard_rows = KV // shards

    key_copies, wk_copies, wv_copies = [], [], []
    for (dz, which), piece in zip(layout, piece_refs):
        for j, (dx, dc) in enumerate(which):
            zz = lax.rem(z + dz + zs, zs)
            xx = 1 - xh if dx else xh
            cc = 1 - core if dc else core
            shard, n = (zz * 2 + xx) * 2 + cc, len(key_copies)
            rows = w_ref.shape[2]
            for i, w_copies in enumerate((wk_copies, wv_copies)):
                src = piece.at[j, pl.ds(latent_rows + i * rows, rows)]
                w_copies.append(
                    pltpu.make_async_copy(src, w_ref.at[i, shard], w_sem.at[i, n])
                )
            place = span_ref[2 * shard]
            key_rows = pl.ds(0, latent_rows)
            key_copies.append(
                pltpu.make_async_copy(piece.at[j, key_rows], key_ref.at[place], key_sem.at[n])
            )
    for copy in wk_copies + key_copies + wv_copies:
        copy.start()
    for copy in wk_copies:
        copy.wait()

    for h in range(heads):
        rows = slice(h * SPAN, (h + 1) * SPAN)
        at = h * (NOPE + ROPE)
        wk = head_rows(w_ref, 0, h * shard_rows, shard_rows)
        q_latent = dot_t(query_ref[:, at : at + NOPE], wk).astype(jnp.bfloat16)
        q_rope = query_ref[:, at + NOPE : at + NOPE + ROPE]
        for slot in range(2):
            toks = slice(slot * SPAN, (slot + 1) * SPAN)
            q_ref[slot, rows, :KV] = q_latent[toks, :]
            q_ref[slot, rows, KV:] = q_rope[toks, :]

    for copy in key_copies:
        copy.wait()
    for i in range(0, shards, 2):
        left, right = key_ref[i], key_ref[i + 1]
        cols = slice(i * SPAN, (i + 2) * SPAN)
        lo_ref[:, cols] = jnp.concatenate([left[:, :SPAN], right[:, :SPAN]], axis=1)
        hi_ref[:, cols] = jnp.concatenate([left[:, SPAN:], right[:, SPAN:]], axis=1)

    c = span_ref[slot0]
    group = lax.div(c, shards // VARIANTS)
    for variant in range(VARIANTS):

        @pl.when(group == variant)
        def _():
            def body(i, carry):
                rows = pl.ds(pl.multiple_of(i * tile, tile), tile)
                for slot in range(2):
                    attend_rows(q_ref, lo_ref, hi_ref, mix_ref, c, slot, rows, variant)
                return carry

            lax.fori_loop(0, heads * SPAN // tile, body, 0)

    for copy in wv_copies:
        copy.wait()
    for h in range(heads):
        cols = slice(h * VDIM, (h + 1) * VDIM)
        rows = slice(h * SPAN, (h + 1) * SPAN)
        both = jnp.concatenate([mix_ref[0, rows, :], mix_ref[1, rows, :]], axis=0)
        wv = head_rows(w_ref, 1, h * shard_rows, shard_rows)
        out_ref[:, cols] = dot(both, wv).astype(jnp.bfloat16)


def attention(layout, heads, idx, span_ids, query, pieces):
    rows, cols = heads * SPAN, heads * VDIM
    b16 = jnp.bfloat16
    shards = sum(p.shape[0] for p in pieces)
    args = [idx, span_ids, query, *pieces]
    size = sum(math.prod(a.shape) * a.dtype.itemsize for a in args)
    work = 2 * rows * shards * SPAN * 5 // 4
    vmem = pl.BlockSpec(memory_space=pltpu.VMEM)
    return pl.pallas_call(
        functools.partial(attention_kernel, layout, heads, min(rows, 256)),
        out_shape=jax.ShapeDtypeStruct((2 * SPAN, cols), b16),
        in_specs=[pl.BlockSpec(memory_space=pltpu.SMEM)] * 2
        + [vmem]
        + [pl.BlockSpec(memory_space=pltpu.HBM)] * len(pieces),
        out_specs=vmem,
        scratch_shapes=[
            pltpu.VMEM((shards, KV + ROPE, 2 * SPAN), b16),
            pltpu.VMEM((2, shards, (pieces[0].shape[1] - KV - ROPE) // 2, LANES), b16),
            pltpu.VMEM((KV + ROPE, shards * SPAN), b16),
            pltpu.VMEM((KV + ROPE, shards * SPAN), b16),
            pltpu.VMEM((2, rows, KV + ROPE), b16),
            pltpu.VMEM((2, rows, KV), b16),
            pltpu.SemaphoreType.DMA((shards,)),
            pltpu.SemaphoreType.DMA((2, shards)),
        ],
        compiler_params=pltpu.CompilerParams(vmem_limit_bytes=36 << 20),
        cost_estimate=pl.CostEstimate(
            flops=2 * work * (2 * KV + ROPE), bytes_accessed=size, transcendentals=work
        ),
    )(*args)


def per_device(compressed, latent, w_uq, w_uk, w_uv, span_ids):
    toks = compressed.shape[0]
    heads = w_uk.shape[1] // NOPE
    zs, ys, xls = (lax.axis_size(a) for a in ("z", "y", "xl"))
    ctx = lax.axis_index(("z", "xh", "core"))
    idx = jnp.stack([lax.axis_index("z"), lax.axis_index("xh"), lax.axis_index("core"), 2 * ctx])

    own = latent.T
    across = lax.ppermute(own, ("xh", "xl"), [(0, 3), (3, 0), (1, 2), (2, 1)])
    weights = jnp.concatenate([by_head(w_uk), by_head(w_uv)], axis=0)
    weights_x = shift(weights, "xh", 1)
    here = jnp.stack(
        [jnp.concatenate([own, weights], axis=0), jnp.concatenate([across, weights_x], axis=0)]
    )

    copies = jnp.broadcast_to(compressed.T[None], (ys * xls,) + compressed.T.shape)
    (copies,) = gate([copies], here, idx)
    features = lax.all_to_all(copies, ("y", "xl"), 0, 0, tiled=True).reshape(-1, toks)
    query = lax.dot_general(
        features, w_uq, (((0,), (0,)), ((), ())), preferred_element_type=jnp.float32
    ).astype(jnp.bfloat16)

    both, first_xh, second_xh = ((0, 0), (1, 0)), ((0, 0),), ((1, 0),)
    hand = lambda some: [
        (dz, tuple((dx, 1) for dx, _ in which), shift(piece, "core", 1))
        for dz, which, piece in some
    ]
    half = zs // 2
    pieces, late = [(0, both, here)], []
    ahead = behind = here
    for k in range(1, half):
        ahead, behind = shift(ahead, "z", 1), shift(behind, "z", -1)
        if k == half - 2:
            ahead, behind = gate([ahead, behind], query)
        (pieces if k < half - 2 else late).extend([(-k, both, ahead), (k, both, behind)])
    pieces += hand(pieces)
    last = gate([ahead[:1], behind[1:]], *(piece for _, _, piece in pieces[len(pieces) // 2 :]))
    moved = gate([piece for _, _, piece in late], *last)
    late = [(dz, which, piece) for (dz, which, _), piece in zip(late, moved)]
    last = [shift(last[0], "z", 1), shift(last[1], "z", -1)]
    late += [(-half, first_xh, last[0]), (half, second_xh, last[1])]
    pieces += late + hand(late)
    layout = tuple((dz, which) for dz, which, _ in pieces)
    return attention(layout, heads, idx, span_ids, query, [p for _, _, p in pieces])


def solution(mesh):
    fine = Mesh(mesh.devices.reshape(8, 2, 2, 4, 2), ("z", "xh", "core", "y", "xl"))
    ctx, tp = ("z", "xh", "core"), ("y", "xl")
    placed = (P(ctx, tp), P(ctx, None), P(None, tp), P(ctx, tp), P(ctx, tp), P())
    return jax.shard_map(
        per_device, mesh=fine, in_specs=placed, out_specs=P(ctx, tp), check_vma=False
    )
```

```python
import functools
import math

import jax
import jax.numpy as jnp
from jax import lax
from jax.experimental import pallas as pl
from jax.experimental.pallas import tpu as pltpu
from jax.sharding import Mesh, PartitionSpec as P

NOPE = 128
ROPE = 64
VDIM = 128
KV = 512
SPAN = 64
LANES = 128
VARIANTS = 4
MASKED = -1e30
EXP2_SCALE = (NOPE + ROPE) ** (-0.5) * math.log2(math.e)


def gate(values, *done):
    hbm = pl.BlockSpec(memory_space=pl.ANY)
    n = len(values)
    return pl.pallas_call(
        lambda *refs: None,
        out_shape=[jax.ShapeDtypeStruct(v.shape, v.dtype) for v in values],
        in_specs=[hbm] * (n + len(done)),
        out_specs=[hbm] * n,
        input_output_aliases={i: i for i in range(n)},
        compiler_params=pltpu.CompilerParams(vmem_limit_bytes=1 << 20),
        cost_estimate=pl.CostEstimate(flops=0, bytes_accessed=0, transcendentals=0),
    )(*values, *done)


def shift(x, axis, by):
    n = lax.axis_size(axis)
    return lax.ppermute(x, axis, [(i, (i + by) % n) for i in range(n)])


def dot(a, b):
    return jnp.dot(a, b, preferred_element_type=jnp.float32)


def dot_t(a, b):
    return lax.dot_general(a, b, (((1,), (1,)), ((), ())), preferred_element_type=jnp.float32)


def by_head(w):
    rows, cols = w.shape
    return w.reshape(rows, cols // LANES, LANES).transpose(1, 0, 2).reshape(-1, LANES)


def head_rows(w_ref, which, at, rows):
    shards = range(w_ref.shape[1])
    return jnp.concatenate([w_ref[which, i, at : at + rows, :] for i in shards], axis=0)


def attend_rows(q_ref, lo_ref, hi_ref, mix_ref, c, slot, rows, variant):
    q = q_ref[slot, rows, :]
    count = lo_ref.shape[1]
    step = count // VARIANTS
    within = lax.broadcasted_iota(jnp.int32, (q.shape[0], 1), 0) % SPAN
    lane = lax.broadcasted_iota(jnp.int32, (1, step), 1)
    if slot == 0:
        open_lo, n_lo = step * variant, step * (variant + 1)
        s_lo = dot(q, lo_ref[:, :n_lo])
        seen = lane + open_lo <= c * SPAN + within
        parts = [jnp.where(seen, s_lo[:, open_lo:], MASKED)]
        if open_lo:
            parts = [s_lo[:, :open_lo]] + parts
    else:
        first = step * variant
        s_hi = dot(q, hi_ref[:, first:])
        at = lane % SPAN - (lane + first) // SPAN * SPAN
        seen = at <= within - c * SPAN
        parts = [dot(q, lo_ref[...]), jnp.where(seen, s_hi[:, :step], MASKED)]
        if first + step < count:
            parts.append(s_hi[:, step:])
    s = jnp.concatenate(parts, axis=1)
    high = jnp.max(s, axis=1, keepdims=True)
    w = jnp.exp2((s - high) * EXP2_SCALE)
    total = jnp.sum(w, axis=1, keepdims=True)
    w = w.astype(jnp.bfloat16)
    if slot == 0:
        acc = dot_t(w, lo_ref[:KV, :n_lo])
    else:
        acc = dot_t(w[:, :count], lo_ref[:KV, :]) + dot_t(w[:, count:], hi_ref[:KV, first:])
    mix_ref[slot, rows, :] = (acc / total).astype(jnp.bfloat16)


def attention_kernel(layout, heads, tile, *refs):
    refs = list(refs)
    take = lambda n: [refs.pop(0) for _ in range(n)]
    idx_ref, span_ref, query_ref = take(3)
    piece_refs = take(len(layout))
    out_ref, key_ref, w_ref, lo_ref, hi_ref, q_ref, mix_ref = refs
    z, xh, core, slot0 = (idx_ref[i] for i in range(4))
    shards, latent_rows = key_ref.shape[:2]
    zs = shards // 4
    shard_rows = KV // shards

    parts, w_rows = 4, w_ref.shape[2]

    def sort(part, carry):
        def quarter(rows):
            size = rows // parts
            return pl.ds(pl.multiple_of(part * size, size), size), size

        keys, _ = quarter(latent_rows)
        some, size = quarter(w_rows)
        for (dz, which), piece in zip(layout, piece_refs):
            for j, (dx, dc) in enumerate(which):
                zz = lax.rem(z + dz + zs, zs)
                xx = 1 - xh if dx else xh
                cc = 1 - core if dc else core
                shard = (zz * 2 + xx) * 2 + cc
                key_ref[span_ref[2 * shard], keys, :] = piece[j, keys, :]
                for i in range(2):
                    at = pl.multiple_of(latent_rows + i * w_rows + part * size, size)
                    w_ref[i, shard, some, :] = piece[j, pl.ds(at, size), :]
        return carry

    lax.fori_loop(0, parts, sort, 0)

    for h in range(heads):
        rows = slice(h * SPAN, (h + 1) * SPAN)
        at = h * (NOPE + ROPE)
        wk = head_rows(w_ref, 0, h * shard_rows, shard_rows)
        q_latent = dot_t(query_ref[:, at : at + NOPE], wk).astype(jnp.bfloat16)
        q_rope = query_ref[:, at + NOPE : at + NOPE + ROPE]
        for slot in range(2):
            toks = slice(slot * SPAN, (slot + 1) * SPAN)
            q_ref[slot, rows, :KV] = q_latent[toks, :]
            q_ref[slot, rows, KV:] = q_rope[toks, :]

    for i in range(0, shards, 2):
        left, right = key_ref[i], key_ref[i + 1]
        cols = slice(i * SPAN, (i + 2) * SPAN)
        lo_ref[:, cols] = jnp.concatenate([left[:, :SPAN], right[:, :SPAN]], axis=1)
        hi_ref[:, cols] = jnp.concatenate([left[:, SPAN:], right[:, SPAN:]], axis=1)

    c = span_ref[slot0]
    group = lax.div(c, shards // VARIANTS)
    for variant in range(VARIANTS):

        @pl.when(group == variant)
        def _():
            def body(i, carry):
                rows = pl.ds(pl.multiple_of(i * tile, tile), tile)
                for slot in range(2):
                    attend_rows(q_ref, lo_ref, hi_ref, mix_ref, c, slot, rows, variant)
                return carry

            lax.fori_loop(0, heads * SPAN // tile, body, 0)

    for h in range(heads):
        cols = slice(h * VDIM, (h + 1) * VDIM)
        rows = slice(h * SPAN, (h + 1) * SPAN)
        both = jnp.concatenate([mix_ref[0, rows, :], mix_ref[1, rows, :]], axis=0)
        wv = head_rows(w_ref, 1, h * shard_rows, shard_rows)
        out_ref[:, cols] = dot(both, wv).astype(jnp.bfloat16)


def attention(layout, heads, idx, span_ids, query, pieces):
    rows, cols = heads * SPAN, heads * VDIM
    b16 = jnp.bfloat16
    shards = sum(p.shape[0] for p in pieces)
    args = [idx, span_ids, query, *pieces]
    size = sum(math.prod(a.shape) * a.dtype.itemsize for a in args)
    work = 2 * rows * shards * SPAN * 5 // 4
    vmem = pl.BlockSpec(memory_space=pltpu.VMEM)
    return pl.pallas_call(
        functools.partial(attention_kernel, layout, heads, min(rows, 256)),
        out_shape=jax.ShapeDtypeStruct((2 * SPAN, cols), b16),
        in_specs=[pl.BlockSpec(memory_space=pltpu.SMEM)] * 2
        + [vmem]
        + [vmem] * len(pieces),
        out_specs=vmem,
        scratch_shapes=[
            pltpu.VMEM((shards, KV + ROPE, 2 * SPAN), b16),
            pltpu.VMEM((2, shards, (pieces[0].shape[1] - KV - ROPE) // 2, LANES), b16),
            pltpu.VMEM((KV + ROPE, shards * SPAN), b16),
            pltpu.VMEM((KV + ROPE, shards * SPAN), b16),
            pltpu.VMEM((2, rows, KV + ROPE), b16),
            pltpu.VMEM((2, rows, KV), b16),
        ],
        compiler_params=pltpu.CompilerParams(vmem_limit_bytes=36 << 20),
        cost_estimate=pl.CostEstimate(
            flops=2 * work * (2 * KV + ROPE), bytes_accessed=size, transcendentals=work
        ),
    )(*args)


def per_device(compressed, latent, w_uq, w_uk, w_uv, span_ids):
    toks = compressed.shape[0]
    heads = w_uk.shape[1] // NOPE
    zs, ys, xls = (lax.axis_size(a) for a in ("z", "y", "xl"))
    ctx = lax.axis_index(("z", "xh", "core"))
    idx = jnp.stack([lax.axis_index("z"), lax.axis_index("xh"), lax.axis_index("core"), 2 * ctx])

    own = latent.T
    across = lax.ppermute(own, ("xh", "xl"), [(0, 3), (3, 0), (1, 2), (2, 1)])
    weights = jnp.concatenate([by_head(w_uk), by_head(w_uv)], axis=0)
    weights_x = shift(weights, "xh", 1)
    here = jnp.stack(
        [jnp.concatenate([own, weights], axis=0), jnp.concatenate([across, weights_x], axis=0)]
    )

    copies = jnp.broadcast_to(compressed.T[None], (ys * xls,) + compressed.T.shape)
    (copies,) = gate([copies], here, idx)
    features = lax.all_to_all(copies, ("y", "xl"), 0, 0, tiled=True).reshape(-1, toks)
    query = lax.dot_general(
        features, w_uq, (((0,), (0,)), ((), ())), preferred_element_type=jnp.float32
    ).astype(jnp.bfloat16)

    both, first_xh, second_xh = ((0, 0), (1, 0)), ((0, 0),), ((1, 0),)
    hand = lambda some: [
        (dz, tuple((dx, 1) for dx, _ in which), shift(piece, "core", 1))
        for dz, which, piece in some
    ]
    half = zs // 2
    pieces, late = [(0, both, here)], []
    ahead = behind = here
    for k in range(1, half):
        ahead, behind = shift(ahead, "z", 1), shift(behind, "z", -1)
        if k == half - 2:
            ahead, behind = gate([ahead, behind], query)
        (pieces if k < half - 2 else late).extend([(-k, both, ahead), (k, both, behind)])
    pieces += hand(pieces)
    last = gate([ahead[:1], behind[1:]], *(piece for _, _, piece in pieces[len(pieces) // 2 :]))
    moved = gate([piece for _, _, piece in late], *last)
    late = [(dz, which, piece) for (dz, which, _), piece in zip(late, moved)]
    last = [shift(last[0], "z", 1), shift(last[1], "z", -1)]
    late += [(-half, first_xh, last[0]), (half, second_xh, last[1])]
    pieces += late + hand(late)
    layout = tuple((dz, which) for dz, which, _ in pieces)
    return attention(layout, heads, idx, span_ids, query, [p for _, _, p in pieces])


def solution(mesh):
    fine = Mesh(mesh.devices.reshape(8, 2, 2, 4, 2), ("z", "xh", "core", "y", "xl"))
    ctx, tp = ("z", "xh", "core"), ("y", "xl")
    placed = (P(ctx, tp), P(ctx, None), P(None, tp), P(ctx, tp), P(ctx, tp), P())
    return jax.shard_map(
        per_device, mesh=fine, in_specs=placed, out_specs=P(ctx, tp), check_vma=False
    )
```

```python
import functools
import math

import jax
import jax.numpy as jnp
from jax import lax
from jax.experimental import pallas as pl
from jax.experimental.pallas import tpu as pltpu
from jax.sharding import Mesh, PartitionSpec as P

NOPE = 128
ROPE = 64
VDIM = 128
KV = 512
SPAN = 64
LANES = 128
VARIANTS = 4
MASKED = -1e30
EXP2_SCALE = (NOPE + ROPE) ** (-0.5) * math.log2(math.e)


def gate(values, *done):
    hbm = pl.BlockSpec(memory_space=pl.ANY)
    n = len(values)
    return pl.pallas_call(
        lambda *refs: None,
        out_shape=[jax.ShapeDtypeStruct(v.shape, v.dtype) for v in values],
        in_specs=[hbm] * (n + len(done)),
        out_specs=[hbm] * n,
        input_output_aliases={i: i for i in range(n)},
        compiler_params=pltpu.CompilerParams(vmem_limit_bytes=1 << 20),
        cost_estimate=pl.CostEstimate(flops=0, bytes_accessed=0, transcendentals=0),
    )(*values, *done)


def shift(x, axis, by):
    n = lax.axis_size(axis)
    return lax.ppermute(x, axis, [(i, (i + by) % n) for i in range(n)])


def dot(a, b):
    return jnp.dot(a, b, preferred_element_type=jnp.float32)


def dot_t(a, b):
    return lax.dot_general(a, b, (((1,), (1,)), ((), ())), preferred_element_type=jnp.float32)


def by_head(w):
    rows, cols = w.shape
    return w.reshape(rows, cols // LANES, LANES).transpose(1, 0, 2).reshape(-1, LANES)


def head_rows(w_ref, which, at, rows):
    shards = range(w_ref.shape[1])
    return jnp.concatenate([w_ref[which, i, at : at + rows, :] for i in shards], axis=0)


def attend_rows(q_ref, lo_ref, hi_ref, mix_ref, c, slot, rows, variant):
    q = q_ref[slot, rows, :]
    count = lo_ref.shape[1]
    step = count // VARIANTS
    within = lax.broadcasted_iota(jnp.int32, (q.shape[0], 1), 0) % SPAN
    lane = lax.broadcasted_iota(jnp.int32, (1, step), 1)
    if slot == 0:
        open_lo, n_lo = step * variant, step * (variant + 1)
        s_lo = dot(q, lo_ref[:, :n_lo])
        seen = lane + open_lo <= c * SPAN + within
        parts = [jnp.where(seen, s_lo[:, open_lo:], MASKED)]
        if open_lo:
            parts = [s_lo[:, :open_lo]] + parts
    else:
        first = step * variant
        s_hi = dot(q, hi_ref[:, first:])
        at = lane % SPAN - (lane + first) // SPAN * SPAN
        seen = at <= within - c * SPAN
        parts = [dot(q, lo_ref[...]), jnp.where(seen, s_hi[:, :step], MASKED)]
        if first + step < count:
            parts.append(s_hi[:, step:])
    s = jnp.concatenate(parts, axis=1)
    high = jnp.max(s, axis=1, keepdims=True)
    w = jnp.exp2((s - high) * EXP2_SCALE)
    total = jnp.sum(w, axis=1, keepdims=True)
    w = w.astype(jnp.bfloat16)
    if slot == 0:
        acc = dot_t(w, lo_ref[:KV, :n_lo])
    else:
        acc = dot_t(w[:, :count], lo_ref[:KV, :]) + dot_t(w[:, count:], hi_ref[:KV, first:])
    mix_ref[slot, rows, :] = (acc / total).astype(jnp.bfloat16)


def attention_kernel(layout, heads, tile, *refs):
    refs = list(refs)
    take = lambda n: [refs.pop(0) for _ in range(n)]
    idx_ref, span_ref, query_ref = take(3)
    piece_refs = take(len(layout))
    out_ref, key_ref, w_ref, lo_ref, hi_ref, q_ref, mix_ref = refs
    z, xh, core, slot0 = (idx_ref[i] for i in range(4))
    shards, latent_rows = key_ref.shape[:2]
    zs = shards // 4
    shard_rows = KV // shards

    moves = []
    for (dz, which), piece in zip(layout, piece_refs):
        zz = lax.rem(z + dz + zs, zs)
        for j, (dx, dc) in enumerate(which):
            xx = 1 - xh if dx else xh
            cc = 1 - core if dc else core
            shard = (zz * 2 + xx) * 2 + cc
            moves.append((piece, j, shard, span_ref[2 * shard]))
    parts, w_rows = 2, w_ref.shape[2]
    key_size, w_size = latent_rows // parts, w_rows // parts

    def sort(part, carry):
        keys = pl.ds(pl.multiple_of(part * key_size, key_size), key_size)
        some = pl.ds(pl.multiple_of(part * w_size, w_size), w_size)
        for piece, j, shard, place in moves:
            key_ref[place, keys, :] = piece[j, keys, :]
            for i in range(2):
                at = pl.multiple_of(latent_rows + i * w_rows + part * w_size, w_size)
                w_ref[i, shard, some, :] = piece[j, pl.ds(at, w_size), :]
        return carry

    lax.fori_loop(0, parts, sort, 0)

    for h in range(heads):
        rows = slice(h * SPAN, (h + 1) * SPAN)
        at = h * (NOPE + ROPE)
        wk = head_rows(w_ref, 0, h * shard_rows, shard_rows)
        q_latent = dot_t(query_ref[:, at : at + NOPE], wk).astype(jnp.bfloat16)
        q_rope = query_ref[:, at + NOPE : at + NOPE + ROPE]
        for slot in range(2):
            toks = slice(slot * SPAN, (slot + 1) * SPAN)
            q_ref[slot, rows, :KV] = q_latent[toks, :]
            q_ref[slot, rows, KV:] = q_rope[toks, :]

    for i in range(0, shards, 2):
        left, right = key_ref[i], key_ref[i + 1]
        cols = slice(i * SPAN, (i + 2) * SPAN)
        lo_ref[:, cols] = jnp.concatenate([left[:, :SPAN], right[:, :SPAN]], axis=1)
        hi_ref[:, cols] = jnp.concatenate([left[:, SPAN:], right[:, SPAN:]], axis=1)

    c = span_ref[slot0]
    group = lax.div(c, shards // VARIANTS)
    for variant in range(VARIANTS):

        @pl.when(group == variant)
        def _():
            def body(i, carry):
                rows = pl.ds(pl.multiple_of(i * tile, tile), tile)
                for slot in range(2):
                    attend_rows(q_ref, lo_ref, hi_ref, mix_ref, c, slot, rows, variant)
                return carry

            lax.fori_loop(0, heads * SPAN // tile, body, 0)

    for h in range(heads):
        cols = slice(h * VDIM, (h + 1) * VDIM)
        rows = slice(h * SPAN, (h + 1) * SPAN)
        both = jnp.concatenate([mix_ref[0, rows, :], mix_ref[1, rows, :]], axis=0)
        wv = head_rows(w_ref, 1, h * shard_rows, shard_rows)
        out_ref[:, cols] = dot(both, wv).astype(jnp.bfloat16)


def attention(layout, heads, idx, span_ids, query, pieces):
    rows, cols = heads * SPAN, heads * VDIM
    b16 = jnp.bfloat16
    shards = sum(p.shape[0] for p in pieces)
    args = [idx, span_ids, query, *pieces]
    size = sum(math.prod(a.shape) * a.dtype.itemsize for a in args)
    work = 2 * rows * shards * SPAN * 5 // 4
    vmem = pl.BlockSpec(memory_space=pltpu.VMEM)
    return pl.pallas_call(
        functools.partial(attention_kernel, layout, heads, min(rows, 256)),
        out_shape=jax.ShapeDtypeStruct((2 * SPAN, cols), b16),
        in_specs=[pl.BlockSpec(memory_space=pltpu.SMEM)] * 2
        + [vmem]
        + [vmem] * len(pieces),
        out_specs=vmem,
        scratch_shapes=[
            pltpu.VMEM((shards, KV + ROPE, 2 * SPAN), b16),
            pltpu.VMEM((2, shards, (pieces[0].shape[1] - KV - ROPE) // 2, LANES), b16),
            pltpu.VMEM((KV + ROPE, shards * SPAN), b16),
            pltpu.VMEM((KV + ROPE, shards * SPAN), b16),
            pltpu.VMEM((2, rows, KV + ROPE), b16),
            pltpu.VMEM((2, rows, KV), b16),
        ],
        compiler_params=pltpu.CompilerParams(vmem_limit_bytes=36 << 20),
        cost_estimate=pl.CostEstimate(
            flops=2 * work * (2 * KV + ROPE), bytes_accessed=size, transcendentals=work
        ),
    )(*args)


def per_device(compressed, latent, w_uq, w_uk, w_uv, span_ids):
    toks = compressed.shape[0]
    heads = w_uk.shape[1] // NOPE
    zs, ys, xls = (lax.axis_size(a) for a in ("z", "y", "xl"))
    ctx = lax.axis_index(("z", "xh", "core"))
    idx = jnp.stack([lax.axis_index("z"), lax.axis_index("xh"), lax.axis_index("core"), 2 * ctx])

    own = latent.T
    across = lax.ppermute(own, ("xh", "xl"), [(0, 3), (3, 0), (1, 2), (2, 1)])
    weights = jnp.concatenate([by_head(w_uk), by_head(w_uv)], axis=0)
    weights_x = shift(weights, "xh", 1)
    here = jnp.stack(
        [jnp.concatenate([own, weights], axis=0), jnp.concatenate([across, weights_x], axis=0)]
    )

    copies = jnp.broadcast_to(compressed.T[None], (ys * xls,) + compressed.T.shape)
    (copies,) = gate([copies], here, idx)
    features = lax.all_to_all(copies, ("y", "xl"), 0, 0, tiled=True).reshape(-1, toks)
    query = lax.dot_general(
        features, w_uq, (((0,), (0,)), ((), ())), preferred_element_type=jnp.float32
    ).astype(jnp.bfloat16)

    both, first_xh, second_xh = ((0, 0), (1, 0)), ((0, 0),), ((1, 0),)
    hand = lambda some: [
        (dz, tuple((dx, 1) for dx, _ in which), shift(piece, "core", 1))
        for dz, which, piece in some
    ]
    half = zs // 2
    pieces, late = [(0, both, here)], []
    ahead = behind = here
    for k in range(1, half):
        ahead, behind = shift(ahead, "z", 1), shift(behind, "z", -1)
        if k == half - 2:
            ahead, behind = gate([ahead, behind], query)
        (pieces if k < half - 2 else late).extend([(-k, both, ahead), (k, both, behind)])
    pieces += hand(pieces)
    last = gate([ahead[:1], behind[1:]], *(piece for _, _, piece in pieces[len(pieces) // 2 :]))
    moved = gate([piece for _, _, piece in late], *last)
    late = [(dz, which, piece) for (dz, which, _), piece in zip(late, moved)]
    last = [shift(last[0], "z", 1), shift(last[1], "z", -1)]
    late += [(-half, first_xh, last[0]), (half, second_xh, last[1])]
    pieces += late + hand(late)
    layout = tuple((dz, which) for dz, which, _ in pieces)
    return attention(layout, heads, idx, span_ids, query, [p for _, _, p in pieces])


def solution(mesh):
    fine = Mesh(mesh.devices.reshape(8, 2, 2, 4, 2), ("z", "xh", "core", "y", "xl"))
    ctx, tp = ("z", "xh", "core"), ("y", "xl")
    placed = (P(ctx, tp), P(ctx, None), P(None, tp), P(ctx, tp), P(ctx, tp), P())
    return jax.shard_map(
        per_device, mesh=fine, in_specs=placed, out_specs=P(ctx, tp), check_vma=False
    )
```

```python
import functools
import math

import jax
import jax.numpy as jnp
from jax import lax
from jax.experimental import pallas as pl
from jax.experimental.pallas import tpu as pltpu
from jax.sharding import Mesh, PartitionSpec as P

NOPE = 128
ROPE = 64
VDIM = 128
KV = 512
SPAN = 64
LANES = 128
VARIANTS = 4
MASKED = -1e30
EXP2_SCALE = (NOPE + ROPE) ** (-0.5) * math.log2(math.e)


def gate(values, *done):
    hbm = pl.BlockSpec(memory_space=pl.ANY)
    n = len(values)
    return pl.pallas_call(
        lambda *refs: None,
        out_shape=[jax.ShapeDtypeStruct(v.shape, v.dtype) for v in values],
        in_specs=[hbm] * (n + len(done)),
        out_specs=[hbm] * n,
        input_output_aliases={i: i for i in range(n)},
        compiler_params=pltpu.CompilerParams(vmem_limit_bytes=1 << 20),
        cost_estimate=pl.CostEstimate(flops=0, bytes_accessed=0, transcendentals=0),
    )(*values, *done)


def shift(x, axis, by):
    n = lax.axis_size(axis)
    return lax.ppermute(x, axis, [(i, (i + by) % n) for i in range(n)])


def dot(a, b):
    return jnp.dot(a, b, preferred_element_type=jnp.float32)


def dot_t(a, b):
    return lax.dot_general(a, b, (((1,), (1,)), ((), ())), preferred_element_type=jnp.float32)


def by_head(w):
    rows, cols = w.shape
    return w.reshape(rows, cols // LANES, LANES).transpose(1, 0, 2).reshape(-1, LANES)


def head_rows(w_ref, which, at, rows):
    shards = range(w_ref.shape[1])
    return jnp.concatenate([w_ref[which, i, at : at + rows, :] for i in shards], axis=0)


def attend_rows(q_ref, lo_ref, hi_ref, mix_ref, c, slot, rows, variant):
    q = q_ref[slot, rows, :]
    count = lo_ref.shape[1]
    step = count // VARIANTS
    within = lax.broadcasted_iota(jnp.int32, (q.shape[0], 1), 0) % SPAN
    lane = lax.broadcasted_iota(jnp.int32, (1, step), 1)
    if slot == 0:
        open_lo, n_lo = step * variant, step * (variant + 1)
        s_lo = dot(q, lo_ref[:, :n_lo])
        seen = lane + open_lo <= c * SPAN + within
        parts = [jnp.where(seen, s_lo[:, open_lo:], MASKED)]
        if open_lo:
            parts = [s_lo[:, :open_lo]] + parts
    else:
        first = step * variant
        s_hi = dot(q, hi_ref[:, first:])
        at = lane % SPAN - (lane + first) // SPAN * SPAN
        seen = at <= within - c * SPAN
        parts = [dot(q, lo_ref[...]), jnp.where(seen, s_hi[:, :step], MASKED)]
        if first + step < count:
            parts.append(s_hi[:, step:])
    s = jnp.concatenate(parts, axis=1)
    high = jnp.max(s, axis=1, keepdims=True)
    w = jnp.exp2((s - high) * EXP2_SCALE)
    total = jnp.sum(w, axis=1, keepdims=True)
    w = w.astype(jnp.bfloat16)
    if slot == 0:
        acc = dot_t(w, lo_ref[:KV, :n_lo])
    else:
        acc = dot_t(w[:, :count], lo_ref[:KV, :]) + dot_t(w[:, count:], hi_ref[:KV, first:])
    mix_ref[slot, rows, :] = (acc * (1.0 / total)).astype(jnp.bfloat16)


def attention_kernel(layout, heads, tile, *refs):
    refs = list(refs)
    take = lambda n: [refs.pop(0) for _ in range(n)]
    idx_ref, span_ref, query_ref = take(3)
    piece_refs = take(len(layout))
    out_ref, key_ref, w_ref, lo_ref, hi_ref, q_ref, mix_ref = refs
    z, xh, core, slot0 = (idx_ref[i] for i in range(4))
    shards, latent_rows = key_ref.shape[:2]
    zs = shards // 4
    shard_rows = KV // shards

    moves = []
    for (dz, which), piece in zip(layout, piece_refs):
        zz = lax.rem(z + dz + zs, zs)
        for j, (dx, dc) in enumerate(which):
            xx = 1 - xh if dx else xh
            cc = 1 - core if dc else core
            shard = (zz * 2 + xx) * 2 + cc
            moves.append((piece, j, shard, span_ref[2 * shard]))
    parts, w_rows = 2, w_ref.shape[2]
    key_size, w_size = latent_rows // parts, w_rows // parts

    def sort(part, carry):
        keys = pl.ds(pl.multiple_of(part * key_size, key_size), key_size)
        some = pl.ds(pl.multiple_of(part * w_size, w_size), w_size)
        for piece, j, shard, place in moves:
            key_ref[place, keys, :] = piece[j, keys, :]
            for i in range(2):
                at = pl.multiple_of(latent_rows + i * w_rows + part * w_size, w_size)
                w_ref[i, shard, some, :] = piece[j, pl.ds(at, w_size), :]
        return carry

    lax.fori_loop(0, parts, sort, 0)

    for h in range(heads):
        rows = slice(h * SPAN, (h + 1) * SPAN)
        at = h * (NOPE + ROPE)
        wk = head_rows(w_ref, 0, h * shard_rows, shard_rows)
        q_latent = dot_t(query_ref[:, at : at + NOPE], wk).astype(jnp.bfloat16)
        q_rope = query_ref[:, at + NOPE : at + NOPE + ROPE]
        for slot in range(2):
            toks = slice(slot * SPAN, (slot + 1) * SPAN)
            q_ref[slot, rows, :KV] = q_latent[toks, :]
            q_ref[slot, rows, KV:] = q_rope[toks, :]

    for i in range(0, shards, 2):
        left, right = key_ref[i], key_ref[i + 1]
        cols = slice(i * SPAN, (i + 2) * SPAN)
        lo_ref[:, cols] = jnp.concatenate([left[:, :SPAN], right[:, :SPAN]], axis=1)
        hi_ref[:, cols] = jnp.concatenate([left[:, SPAN:], right[:, SPAN:]], axis=1)

    c = span_ref[slot0]
    group = lax.div(c, shards // VARIANTS)
    for variant in range(VARIANTS):

        @pl.when(group == variant)
        def _():
            def body(i, carry):
                rows = pl.ds(pl.multiple_of(i * tile, tile), tile)
                for slot in range(2):
                    attend_rows(q_ref, lo_ref, hi_ref, mix_ref, c, slot, rows, variant)
                return carry

            lax.fori_loop(0, heads * SPAN // tile, body, 0)

    for h in range(heads):
        cols = slice(h * VDIM, (h + 1) * VDIM)
        rows = slice(h * SPAN, (h + 1) * SPAN)
        both = jnp.concatenate([mix_ref[0, rows, :], mix_ref[1, rows, :]], axis=0)
        wv = head_rows(w_ref, 1, h * shard_rows, shard_rows)
        out_ref[:, cols] = dot(both, wv).astype(jnp.bfloat16)


def attention(layout, heads, idx, span_ids, query, pieces):
    rows, cols = heads * SPAN, heads * VDIM
    b16 = jnp.bfloat16
    shards = sum(p.shape[0] for p in pieces)
    args = [idx, span_ids, query, *pieces]
    size = sum(math.prod(a.shape) * a.dtype.itemsize for a in args)
    work = 2 * rows * shards * SPAN * 5 // 4
    vmem = pl.BlockSpec(memory_space=pltpu.VMEM)
    return pl.pallas_call(
        functools.partial(attention_kernel, layout, heads, min(rows, 256)),
        out_shape=jax.ShapeDtypeStruct((2 * SPAN, cols), b16),
        in_specs=[pl.BlockSpec(memory_space=pltpu.SMEM)] * 2
        + [vmem]
        + [vmem] * len(pieces),
        out_specs=vmem,
        scratch_shapes=[
            pltpu.VMEM((shards, KV + ROPE, 2 * SPAN), b16),
            pltpu.VMEM((2, shards, (pieces[0].shape[1] - KV - ROPE) // 2, LANES), b16),
            pltpu.VMEM((KV + ROPE, shards * SPAN), b16),
            pltpu.VMEM((KV + ROPE, shards * SPAN), b16),
            pltpu.VMEM((2, rows, KV + ROPE), b16),
            pltpu.VMEM((2, rows, KV), b16),
        ],
        compiler_params=pltpu.CompilerParams(vmem_limit_bytes=36 << 20),
        cost_estimate=pl.CostEstimate(
            flops=2 * work * (2 * KV + ROPE), bytes_accessed=size, transcendentals=work
        ),
    )(*args)


def per_device(compressed, latent, w_uq, w_uk, w_uv, span_ids):
    toks = compressed.shape[0]
    heads = w_uk.shape[1] // NOPE
    zs, ys, xls = (lax.axis_size(a) for a in ("z", "y", "xl"))
    ctx = lax.axis_index(("z", "xh", "core"))
    idx = jnp.stack([lax.axis_index("z"), lax.axis_index("xh"), lax.axis_index("core"), 2 * ctx])

    own = latent.T
    across = lax.ppermute(own, ("xh", "xl"), [(0, 3), (3, 0), (1, 2), (2, 1)])
    weights = jnp.concatenate([by_head(w_uk), by_head(w_uv)], axis=0)
    weights_x = shift(weights, "xh", 1)
    here = jnp.stack(
        [jnp.concatenate([own, weights], axis=0), jnp.concatenate([across, weights_x], axis=0)]
    )

    copies = jnp.broadcast_to(compressed.T[None], (ys * xls,) + compressed.T.shape)
    (copies,) = gate([copies], here, idx)
    features = lax.all_to_all(copies, ("y", "xl"), 0, 0, tiled=True).reshape(-1, toks)
    query = lax.dot_general(
        features, w_uq, (((0,), (0,)), ((), ())), preferred_element_type=jnp.float32
    ).astype(jnp.bfloat16)

    both, first_xh, second_xh = ((0, 0), (1, 0)), ((0, 0),), ((1, 0),)
    hand = lambda some: [
        (dz, tuple((dx, 1) for dx, _ in which), shift(piece, "core", 1))
        for dz, which, piece in some
    ]
    half = zs // 2
    pieces, late = [(0, both, here)], []
    ahead = behind = here
    for k in range(1, half):
        ahead, behind = shift(ahead, "z", 1), shift(behind, "z", -1)
        if k == half - 2:
            ahead, behind = gate([ahead, behind], query)
        (pieces if k < half - 2 else late).extend([(-k, both, ahead), (k, both, behind)])
    pieces += hand(pieces)
    last = gate([ahead[:1], behind[1:]], *(piece for _, _, piece in pieces[len(pieces) // 2 :]))
    moved = gate([piece for _, _, piece in late], *last)
    late = [(dz, which, piece) for (dz, which, _), piece in zip(late, moved)]
    last = [shift(last[0], "z", 1), shift(last[1], "z", -1)]
    late += [(-half, first_xh, last[0]), (half, second_xh, last[1])]
    pieces += late + hand(late)
    layout = tuple((dz, which) for dz, which, _ in pieces)
    return attention(layout, heads, idx, span_ids, query, [p for _, _, p in pieces])


def solution(mesh):
    fine = Mesh(mesh.devices.reshape(8, 2, 2, 4, 2), ("z", "xh", "core", "y", "xl"))
    ctx, tp = ("z", "xh", "core"), ("y", "xl")
    placed = (P(ctx, tp), P(ctx, None), P(None, tp), P(ctx, tp), P(ctx, tp), P())
    return jax.shard_map(
        per_device, mesh=fine, in_specs=placed, out_specs=P(ctx, tp), check_vma=False
    )
```
